32 devices in a mesh: groups: 2 (over y), tm: 4 (over z), space: 4 (over x, core).
Axes of the slice: x: 2, y: 2, z: 4, core: 2. Of those that a mesh axis runs over, the one named last changes fastest.
Arguments:
- start_noise: float32 [16, 128, 128], P(None, ('groups', 'space')), parts along dimension 1, may hold values from -6 to 6
- time_embed: float32 [4, 128], P('tm'), may hold values from -6 to 6
- keep_rate: float32 [4], P('tm'), may hold values from -0.75 to -0.5, as said below
- denoise_rate: float32 [4], P('tm'), may hold values from 0.125 to 0.375, as said below
- conv_first: bfloat16 [9, 128, 16], replicated, may hold values from -1 to 1
- conv_middle: bfloat16 [9, 128, 128], replicated, may hold values from -0.25 to 0.25
- conv_last: bfloat16 [9, 16, 128], replicated, may hold values from -0.1875 to 0.1875
- out_bias: float32 [16], replicated, may hold values from -3 to 3
Outputs:
- trajectory: float32 [4, 16, 128, 128], P('tm', None, ('groups', 'space')), parts along dimension 2
The draws below stay inside these ranges and needn't reach their ends.
There are 2 independent parts, one for each index of `groups`. The reference program is written for one: setup_inputs(seed, part) draws one part's arguments, and reference() takes and returns one part's arrays. A program takes and returns all parts, laid end to end along the dimension named above; an argument that names none is the same for every part. Nothing has to cross between parts.
Inputs may be any that keep to these rules, and one draw needn't show every extreme that they name: `keep_rate`: every entry times 4 lies between -3 and -2. `denoise_rate`: every entry times 4 lies between 0.5 and 1.5.
All inputs are finite; a program needn't handle non-finite values.
Results may differ from the reference program's by a relative error of at most 0.0031.
Values may be sent and summed in bfloat16 or wider, within the bound.
No kernel may reach another device: no remote copies, remote signals or barrier semaphores. Data moves between devices by JAX's collectives and lax.ppermute only.
A program may use at most 64 MiB of HBM per device.

```python
import jax
import jax.numpy as jnp
from jax import lax

CH = 16
HID = 128
W = 128
ITERS = 3
TIMES = 4
NH = 64


def draw_keep_rate(key, part):
    values = jax.random.uniform(key, (TIMES,), jnp.float32, -3.0, -2.0)
    return values / TIMES


def draw_denoise_rate(key, part):
    values = jax.random.uniform(key, (TIMES,), jnp.float32, 0.5, 1.5)
    return values / TIMES


def levels(stream_key, extent, pieces, least, largest):
    loudness = 1.0
    for dim, parts in pieces:
        heights = jax.random.uniform(jax.random.fold_in(jax.random.fold_in(stream_key, 6), dim), (parts,), jnp.float32, least / len(pieces), largest / len(pieces))
        loudness = loudness * jnp.repeat(jnp.exp(heights), extent[dim] // parts).reshape((-1,) + (1,) * (len(extent) - 1 - dim))
    return loudness


def gaussian(rng, dims, spread, reach, shards=(), kind=jnp.bfloat16):
    values = jax.random.normal(rng, dims, jnp.float32) * spread
    if len(shards) > 0:
        values = levels(rng, dims, shards, -0.22, 0.18) * values
    return jnp.clip(values, min=-reach, max=reach).astype(kind)


def setup_inputs(seed: int = 0, part: int = 0) -> dict:
    arg_keys = jax.random.split(jax.random.key(seed), 9)
    part_splits = jax.random.split(jax.random.fold_in(arg_keys[8], part), 9)
    start_noise = gaussian(part_splits[0], (CH, NH, W), 1.0, 6.0, ((1, 4),), jnp.float32)
    time_embed = gaussian(arg_keys[1], (TIMES, HID), 1.0, 6.0, ((0, 4),), jnp.float32)
    keep_rate = draw_keep_rate(jax.random.fold_in(arg_keys[8], 71), part)
    denoise_rate = draw_denoise_rate(jax.random.fold_in(arg_keys[8], 71), part)
    conv_first = gaussian(arg_keys[4], (9, HID, CH), (9 * CH // 4) ** -0.5, 1.0)
    conv_middle = gaussian(arg_keys[5], (9, HID, HID), (9 * HID // 2) ** -0.5, 0.25)
    conv_last = gaussian(arg_keys[6], (9, CH, HID), (9 * HID) ** -0.5, 0.1875)
    out_bias = gaussian(arg_keys[7], (CH,), 0.5, 3.0, (), jnp.float32)
    return dict(start_noise=start_noise, time_embed=time_embed, keep_rate=keep_rate, denoise_rate=denoise_rate, conv_first=conv_first, conv_middle=conv_middle, conv_last=conv_last, out_bias=out_bias)


def convolve(field, taps):
    rows = field.shape[1]
    cols = field.shape[2]
    padded = jnp.pad(field.astype(jnp.float32), ((0, 0), (1, 1), (1, 1)))
    weights = taps.astype(jnp.float32)
    total = jnp.zeros((taps.shape[1], rows, cols), jnp.float32)
    for offset in range(9):
        row_shift = offset // 3
        col_shift = offset % 3
        window = padded[:, row_shift:row_shift + rows, col_shift:col_shift + cols]
        total = total + jnp.einsum("oc,crw->orw", weights[offset], window, precision=lax.Precision.HIGHEST)
    return total


def drift_one(state, embed, keep, rate, conv_first, conv_middle, conv_last, out_bias):
    inputs = state.astype(jnp.bfloat16)
    first = jax.nn.silu(convolve(inputs, conv_first) + embed[:, None, None]).astype(jnp.bfloat16)
    second = jax.nn.silu(convolve(first, conv_middle)).astype(jnp.bfloat16)
    denoised = state + convolve(second, conv_last) + out_bias[:, None, None]
    return keep * state + rate * denoised


def reference(start_noise, time_embed, keep_rate, denoise_rate, conv_first, conv_middle, conv_last, out_bias):
    state = jnp.broadcast_to(start_noise[None], (TIMES,) + start_noise.shape).astype(jnp.float32)
    for step in range(ITERS):
        def one_time(items):
            return drift_one(items[0], items[1], items[2], items[3], conv_first, conv_middle, conv_last, out_bias)

        drift = lax.map(one_time, (state, time_embed, keep_rate, denoise_rate))
        running = jnp.cumsum(drift, axis=0)
        earlier = jnp.concatenate([jnp.zeros_like(drift[:1]), running[:-1]], axis=0)
        state = start_noise[None] + earlier
    return state
```

```python
import jax
import jax.numpy as jnp
from jax import lax
from jax.experimental import pallas as pl
from jax.experimental.pallas import tpu as pltpu
from jax.sharding import PartitionSpec as P

ITERS = 3
HALO = 3 * ITERS
BF16 = jnp.bfloat16
F32 = jnp.float32


def padded(value, sides, width):
    for axis, dim in sides:
        count, length = (lax.axis_size(axis), value.shape[dim])
        up = [(i, (i + 1) % count) for i in range(count - 1)]
        down = [(j, i) for i, j in up]
        last = lax.slice_in_dim(value, length - width, length, axis=dim)
        initial = lax.slice_in_dim(value, 0, width, axis=dim)
        before = lax.ppermute(last, axis, up)
        after = lax.ppermute(initial, axis, down)
        value = jnp.concatenate([before, value, after], axis=dim)
    return value


def carried_in(part, axis):
    place = lax.axis_index(axis)
    gathered = lax.all_gather(part, axis)
    earlier = jnp.arange(gathered.shape[0]) < place
    return jnp.sum(jnp.where(earlier[:, None, None, None], gathered, 0.0), axis=0)


def convolve(field, taps):
    kernel = taps.reshape((3, 3, taps.shape[1], taps.shape[2]))
    result = lax.conv_general_dilated(
        field[None],
        kernel,
        (1, 1),
        ((0, 0), (1, 1)),
        dimension_numbers=("NCHW", "HWOI", "NCHW"),
        preferred_element_type=F32,
    )
    return result[0]


def inside_rows(margin, count, tile_rows):
    glob_row = lax.axis_index("space") * tile_rows - margin + jnp.arange(count, dtype=jnp.int32)
    valid = (glob_row >= 0) & (glob_row < tile_rows * lax.axis_size("space"))
    return valid.astype(F32)[None, :, None]


def picard(
    start_noise, time_embed, keep_rate, denoise_rate, conv_first, conv_middle, conv_last, out_bias
):
    tile_rows = start_noise.shape[1]
    embed = time_embed[0][:, None, None]
    keep = keep_rate[0]
    rate = denoise_rate[0]
    bias = out_bias[:, None, None]
    state = start_noise
    for step in range(ITERS):
        inputs = state.astype(BF16)
        extended = padded(inputs, (("space", 1),), 3)
        first = jax.nn.silu(convolve(extended, conv_first) + embed)
        first = (first * inside_rows(2, tile_rows + 4, tile_rows)).astype(BF16)
        second = jax.nn.silu(convolve(first, conv_middle))
        second = (second * inside_rows(1, tile_rows + 2, tile_rows)).astype(BF16)
        last = convolve(second, conv_last)
        denoised = state + last + bias
        drift = keep * state + rate * denoised
        state = start_noise + carried_in(drift, "tm")
    return state[None]


COLS = 128
GRAIN = 16
PAD = COLS + 2 * GRAIN


def pack_kernel(noise_ref, embed_ref, keep_ref, rate_ref, up_ref, down_ref, far_ref):
    rows = noise_ref.shape[1]
    params = jnp.concatenate(
        [
            embed_ref[...],
            jnp.full((1, COLS), keep_ref[0], F32),
            jnp.full((1, COLS), rate_ref[0], F32),
            jnp.zeros((5, COLS), F32),
        ],
        axis=0,
    )
    full = jnp.concatenate([params, jnp.zeros((8, COLS), F32)], axis=0)
    for i in range(HALO):
        up_ref[i] = noise_ref[:, rows - HALO + i, :]
        down_ref[i] = noise_ref[:, i, :]
    up_ref[HALO] = full
    down_ref[HALO] = full
    far_ref[...] = params


def weights_kernel(first_ref, middle_ref, last_ref, w1a_ref, w1b_ref, wm_ref, w3_ref):
    w1a_ref[...] = jnp.zeros(w1a_ref.shape, BF16)
    w1b_ref[...] = jnp.zeros(w1b_ref.shape, BF16)
    for tap in range(9):
        a, b = divmod(tap, 3)
        block = (first_ref[tap].astype(F32).T * 0.5).astype(BF16)
        for out in range(6):
            row = out + a
            w1a_ref[pl.ds(128 * b + 16 * row, 16), pl.ds(128 * out, 128)] = block
        for out in range(2):
            row = 6 + out + a
            place = row - 8 if row >= 8 else row
            w1b_ref[pl.ds(128 * b + 16 * place, 16), pl.ds(128 * out, 128)] = block
        block = (middle_ref[tap].astype(F32).T * 0.5).astype(BF16)
        for out in range(2):
            wm_ref[pl.ds(512 * b + 128 * (out + a), 128), pl.ds(128 * out, 128)] = block
    zero = jnp.zeros((128, 128), BF16)
    for b in range(3):
        wm_ref[pl.ds(512 * b + 384, 128), pl.ds(0, 128)] = zero
        wm_ref[pl.ds(512 * b, 128), pl.ds(128, 128)] = zero
        for row in range(10):
            parts = []
            for out in range(8):
                a = row - out
                if 0 <= a < 3:
                    parts.append(last_ref[3 * a + b].astype(F32))
                else:
                    parts.append(jnp.zeros((16, 128), F32))
            block = jnp.concatenate(parts, axis=0).T.astype(BF16)
            w3_ref[pl.ds(128 * row, 128), pl.ds(128 * b, 128)] = block


def split3(value):
    high = value.astype(BF16)
    rest = value - high.astype(F32)
    mid = rest.astype(BF16)
    low = (rest - mid.astype(F32)).astype(BF16)
    return high, mid, low


def shifted_rows(grain, by):
    row = lax.broadcasted_iota(jnp.int32, grain.shape, 0)
    if by > 0:
        return jnp.where(row == 0, 0.0, pltpu.roll(grain, 1, 0))
    return jnp.where(row == GRAIN - 1, 0.0, pltpu.roll(grain, GRAIN - 1, 0))


def half_silu(half):
    return half * jnp.tanh(half) + half


def chain_kernel(
    tm_size,
    space_size,
    rows,
    noise_ref,
    before_ref,
    after_ref,
    far_ref,
    place_ref,
    bias_ref,
    w1a_ref,
    w1b_ref,
    wm_ref,
    w3_ref,
    out_ref,
    state_ref,
    zb_ref,
    first_ref,
    second_ref,
):
    time = place_ref[0]
    tile = place_ref[1]
    top = (tile > 0).astype(F32)
    bottom = (tile < space_size - 1).astype(F32)

    w_new = lax.broadcasted_iota(jnp.int32, (COLS, COLS), 0)
    w_old = lax.broadcasted_iota(jnp.int32, (COLS, COLS), 1)
    order = jnp.where(w_old == (w_new % GRAIN) * 8 + w_new // GRAIN, 1.0, 0.0).astype(BF16)
    lane = lax.broadcasted_iota(jnp.int32, (1, COLS), 1)
    lane_row = lane // 16

    def row_scale(rel):
        if rel < 0:
            return top
        if rel >= rows:
            return bottom
        return None

    def lane_scale(tile_index, halo):
        rel = lane_row + (8 * tile_index - halo)
        return jnp.where(rel < 0, top, jnp.where(rel >= rows, bottom, 1.0))

    total = rows + 2 * HALO
    for t in range(pl.cdiv(total, 8)):
        parts = []
        for e in range(8 * t, 8 * t + 8):
            if e < HALO:
                parts.append(before_ref[e])
            elif e < HALO + rows:
                parts.append(noise_ref[:, e - HALO, :])
            elif e < total:
                parts.append(after_ref[e - HALO - rows])
            else:
                parts.append(jnp.zeros((16, COLS), F32))
        block = jnp.concatenate(parts, axis=0)
        moved = None
        for piece in split3(block):
            part = lax.dot_general(
                order, piece, (((1,), (1,)), ((), ())), preferred_element_type=F32
            )
            moved = part if moved is None else moved + part
        state_ref[t] = moved * lane_scale(t, HALO)

    bias = jnp.concatenate([bias_ref[...]] * 8, axis=1)
    params = [far_ref[...], after_ref[HALO], before_ref[HALO]]
    second_ref[...] = jnp.zeros(second_ref.shape, BF16)

    def masked(value, pair, margin):
        halves = []
        scales = [row_scale(2 * pair + i - margin) for i in range(2)]
        if scales[0] is None and scales[1] is None:
            return value
        for i in range(2):
            half = value[:, 128 * i : 128 * (i + 1)]
            halves.append(half if scales[i] is None else half * scales[i])
        return jnp.concatenate(halves, axis=1)

    def keep_first(value, pair, margin):
        value = masked(half_silu(value), pair, margin)
        first_ref[pair, GRAIN : GRAIN + COLS, :] = value.astype(BF16)
        first_ref[pair, 0:GRAIN, :] = shifted_rows(value[COLS - GRAIN :], 1).astype(BF16)
        first_ref[pair, GRAIN + COLS :, :] = shifted_rows(value[:GRAIN], -1).astype(BF16)

    for step in range(ITERS):
        halo = HALO - 3 * step
        count = rows + 2 * halo
        tiles = pl.cdiv(count, 8)
        pairs = (count - 2) // 2
        active = jnp.where(time - ITERS + step >= 0, 1.0, 0.0)
        embed = params[step][0:1] * 0.5
        embed = jnp.concatenate([embed, embed], axis=1)
        keep = params[step][1:2] * active
        rate = params[step][2:3] * active

        for t in range(tiles):
            z = state_ref[t]
            zb_ref[t, GRAIN : GRAIN + COLS, :] = z.astype(BF16)
            zb_ref[t, 0:GRAIN, :] = shifted_rows(z[COLS - GRAIN :], 1).astype(BF16)
            zb_ref[t, GRAIN + COLS :, :] = shifted_rows(z[:GRAIN], -1).astype(BF16)

        def three(t):
            return jnp.concatenate(
                [zb_ref[t, GRAIN * b : GRAIN * b + COLS, :] for b in range(3)], axis=1
            )

        for t in range(tiles):
            here = min(3, pairs - 4 * t)
            if here > 0:
                out = jnp.dot(
                    three(t), w1a_ref[:, : 256 * here], preferred_element_type=F32
                )
                for i in range(here):
                    value = out[:, 256 * i : 256 * (i + 1)] + embed
                    keep_first(value, 4 * t + i, halo - 1)
            if 4 * t + 3 < pairs:
                both = jnp.concatenate([lane < 64] * 3, axis=1)
                out = jnp.dot(
                    jnp.where(both, three(t + 1), three(t)),
                    w1b_ref[...],
                    preferred_element_type=F32,
                )
                keep_first(out + embed, 4 * t + 3, halo - 1)

        chunk = (pairs - 1) // 3
        for start in range(0, pairs - 1, chunk):
            lhs = jnp.concatenate(
                [
                    jnp.concatenate(
                        [
                            first_ref[p + i, GRAIN * b : GRAIN * b + COLS, :]
                            for b in range(3)
                            for i in range(2)
                        ],
                        axis=1,
                    )
                    for p in range(start, start + chunk)
                ],
                axis=0,
            )
            out = jnp.dot(lhs, wm_ref[...], preferred_element_type=F32)
            for i in range(chunk):
                value = masked(
                    half_silu(out[COLS * i : COLS * (i + 1)]), start + i, halo - 2
                )
                second_ref[start + i] = value.astype(BF16)

        new_count = count - 6
        new_tiles = pl.cdiv(new_count, 8)
        lhs = jnp.concatenate(
            [
                jnp.concatenate([second_ref[4 * t + i] for i in range(5)], axis=1)
                for t in range(new_tiles)
            ],
            axis=0,
        )
        out = jnp.dot(lhs, w3_ref[...], preferred_element_type=F32)
        for t in range(new_tiles):
            g = out[COLS * t : COLS * (t + 1)]
            left = g[:, 0:128]
            right = g[:, 256:384]
            left = jnp.concatenate(
                [shifted_rows(left[COLS - GRAIN :], 1), left[: COLS - GRAIN]], axis=0
            )
            right = jnp.concatenate([right[GRAIN:], shifted_rows(right[:GRAIN], -1)], axis=0)
            conv = left + g[:, 128:256] + right
            here = state_ref[t]
            old = jnp.concatenate([here[:, 48:], state_ref[t + 1][:, :48]], axis=1) if (
                t + 1 < tiles
            ) else jnp.concatenate([here[:, 48:], jnp.zeros((COLS, 48), F32)], axis=1)
            new = old + keep * old + rate * (old + conv + bias)
            if step + 1 < ITERS:
                state_ref[t] = new * lane_scale(t, halo - 3)
            else:
                turned = new.T
                moved = None
                for piece in split3(turned):
                    part = jnp.dot(piece, order, preferred_element_type=F32)
                    moved = part if moved is None else moved + part
                for r in range(8):
                    out_ref[0, :, 8 * t + r, :] = moved[16 * r : 16 * r + 16]


def chain(
    start_noise, time_embed, keep_rate, denoise_rate, conv_first, conv_middle, conv_last, out_bias
):
    channels, rows, cols = start_noise.shape
    tm_size = lax.axis_size("tm")
    space_size = lax.axis_size("space")
    vmem = pl.BlockSpec(memory_space=pltpu.VMEM)
    smem = pl.BlockSpec(memory_space=pltpu.SMEM)
    shape = jax.ShapeDtypeStruct

    up, down, far = pl.pallas_call(
        pack_kernel,
        out_shape=(
            shape((HALO + 1, channels, cols), F32),
            shape((HALO + 1, channels, cols), F32),
            shape((8, cols), F32),
        ),
        in_specs=[vmem, vmem, smem, smem],
        out_specs=(vmem, vmem, vmem),
    )(start_noise, time_embed, keep_rate, denoise_rate)

    def moves(times, tiles):
        pairs = []
        for t in range(tm_size):
            for s in range(space_size):
                target = ((t + times) % tm_size) * space_size + (s + tiles) % space_size
                pairs.append((t * space_size + s, target))
        return pairs

    axes = ("tm", "space")
    before = lax.ppermute(up, axes, moves(1, 1))
    after = lax.ppermute(down, axes, moves(2, -1))
    far = lax.ppermute(far, axes, moves(3, 0))

    w1a, w1b, wm, w3 = pl.pallas_call(
        weights_kernel,
        out_shape=(
            shape((384, 768), BF16),
            shape((384, 256), BF16),
            shape((1536, 256), BF16),
            shape((1280, 384), BF16),
        ),
        in_specs=[vmem] * 3,
        out_specs=(vmem,) * 4,
    )(conv_first, conv_middle, conv_last)

    place = jnp.stack([lax.axis_index("tm"), lax.axis_index("space")]).astype(jnp.int32)
    total = rows + 2 * HALO
    pairs = (total - 2) // 2

    def body(*refs):
        chain_kernel(tm_size, space_size, rows, *refs)

    return pl.pallas_call(
        body,
        out_shape=shape((1, channels, rows, cols), F32),
        in_specs=[vmem] * 4 + [smem] + [vmem] * 5,
        out_specs=vmem,
        scratch_shapes=[
            pltpu.VMEM((pl.cdiv(total, 8), COLS, COLS), F32),
            pltpu.VMEM((pl.cdiv(total, 8), PAD, COLS), BF16),
            pltpu.VMEM((pairs, PAD, 256), BF16),
            pltpu.VMEM((pairs + 1, COLS, 256), BF16),
        ],
        compiler_params=pltpu.CompilerParams(vmem_limit_bytes=48 << 20),
    )(start_noise, before, after, far, place, out_bias.reshape(1, channels), w1a, w1b, wm, w3)


def solution(mesh):
    placed = (
        P(None, ("groups", "space"), None),
        P("tm", None),
        P("tm"),
        P("tm"),
        P(),
        P(),
        P(),
        P(),
    )
    return jax.shard_map(
        chain if mesh.shape["tm"] == ITERS + 1 else picard,
        mesh=mesh,
        in_specs=placed,
        out_specs=P("tm", None, ("groups", "space"), None),
        check_vma=False,
    )
```

```python
import jax
import jax.numpy as jnp
from jax import lax
from jax.experimental import pallas as pl
from jax.experimental.pallas import tpu as pltpu
from jax.sharding import PartitionSpec as P

ITERS = 3
HALO = 3 * ITERS
BF16 = jnp.bfloat16
F32 = jnp.float32


def padded(value, sides, width):
    for axis, dim in sides:
        count, length = (lax.axis_size(axis), value.shape[dim])
        up = [(i, (i + 1) % count) for i in range(count - 1)]
        down = [(j, i) for i, j in up]
        last = lax.slice_in_dim(value, length - width, length, axis=dim)
        initial = lax.slice_in_dim(value, 0, width, axis=dim)
        before = lax.ppermute(last, axis, up)
        after = lax.ppermute(initial, axis, down)
        value = jnp.concatenate([before, value, after], axis=dim)
    return value


def carried_in(part, axis):
    place = lax.axis_index(axis)
    gathered = lax.all_gather(part, axis)
    earlier = jnp.arange(gathered.shape[0]) < place
    return jnp.sum(jnp.where(earlier[:, None, None, None], gathered, 0.0), axis=0)


def convolve(field, taps):
    kernel = taps.reshape((3, 3, taps.shape[1], taps.shape[2]))
    result = lax.conv_general_dilated(
        field[None],
        kernel,
        (1, 1),
        ((0, 0), (1, 1)),
        dimension_numbers=("NCHW", "HWOI", "NCHW"),
        preferred_element_type=F32,
    )
    return result[0]


def inside_rows(margin, count, tile_rows):
    glob_row = lax.axis_index("space") * tile_rows - margin + jnp.arange(count, dtype=jnp.int32)
    valid = (glob_row >= 0) & (glob_row < tile_rows * lax.axis_size("space"))
    return valid.astype(F32)[None, :, None]


def picard(
    start_noise, time_embed, keep_rate, denoise_rate, conv_first, conv_middle, conv_last, out_bias
):
    tile_rows = start_noise.shape[1]
    embed = time_embed[0][:, None, None]
    keep = keep_rate[0]
    rate = denoise_rate[0]
    bias = out_bias[:, None, None]
    state = start_noise
    for step in range(ITERS):
        inputs = state.astype(BF16)
        extended = padded(inputs, (("space", 1),), 3)
        first = jax.nn.silu(convolve(extended, conv_first) + embed)
        first = (first * inside_rows(2, tile_rows + 4, tile_rows)).astype(BF16)
        second = jax.nn.silu(convolve(first, conv_middle))
        second = (second * inside_rows(1, tile_rows + 2, tile_rows)).astype(BF16)
        last = convolve(second, conv_last)
        denoised = state + last + bias
        drift = keep * state + rate * denoised
        state = start_noise + carried_in(drift, "tm")
    return state[None]


COLS = 128
GRAIN = 16
PAD = COLS + 2 * GRAIN


def pack_kernel(noise_ref, embed_ref, keep_ref, rate_ref, up_ref, down_ref, far_ref):
    rows = noise_ref.shape[1]
    params = jnp.concatenate(
        [
            embed_ref[...],
            jnp.full((1, COLS), keep_ref[0], F32),
            jnp.full((1, COLS), rate_ref[0], F32),
            jnp.zeros((5, COLS), F32),
        ],
        axis=0,
    )
    full = jnp.concatenate([params, jnp.zeros((8, COLS), F32)], axis=0)
    for i in range(HALO):
        up_ref[i] = noise_ref[:, rows - HALO + i, :]
        down_ref[i] = noise_ref[:, i, :]
    up_ref[HALO] = full
    down_ref[HALO] = full
    far_ref[...] = params


def weights_kernel(
    first_ref, middle_ref, last_ref, bias_in_ref, w1a_ref, w1b_ref, wm_ref, w3_ref, bias_ref
):
    bias_ref[...] = jnp.concatenate([bias_in_ref[...]] * 8, axis=1)
    w1a_ref[...] = jnp.zeros(w1a_ref.shape, BF16)
    w1b_ref[...] = jnp.zeros(w1b_ref.shape, BF16)
    for tap in range(9):
        a, b = divmod(tap, 3)
        block = first_ref[tap] * BF16(0.5)
        for out in range(6):
            row = out + a
            w1a_ref[pl.ds(128 * b + 16 * row, 16), pl.ds(128 * out, 128)] = block
        for out in range(2):
            row = 6 + out + a
            place = row - 8 if row >= 8 else row
            w1b_ref[pl.ds(128 * b + 16 * place, 16), pl.ds(128 * out, 128)] = block
        block = (middle_ref[tap].astype(F32).T * 0.5).astype(BF16)
        for out in range(2):
            wm_ref[pl.ds(512 * b + 128 * (out + a), 128), pl.ds(128 * out, 128)] = block
    zero = jnp.zeros((128, 128), BF16)
    for b in range(3):
        wm_ref[pl.ds(512 * b + 384, 128), pl.ds(0, 128)] = zero
        wm_ref[pl.ds(512 * b, 128), pl.ds(128, 128)] = zero
        for row in range(10):
            parts = []
            for out in range(8):
                a = row - out
                if 0 <= a < 3:
                    parts.append(last_ref[3 * a + b].astype(F32))
                else:
                    parts.append(jnp.zeros((16, 128), F32))
            block = jnp.concatenate(parts, axis=0).T.astype(BF16)
            w3_ref[pl.ds(128 * row, 128), pl.ds(128 * b, 128)] = block


def split3(value):
    high = value.astype(BF16)
    rest = value - high.astype(F32)
    mid = rest.astype(BF16)
    low = (rest - mid.astype(F32)).astype(BF16)
    return high, mid, low


def shifted_rows(grain, by):
    row = lax.broadcasted_iota(jnp.int32, grain.shape, 0)
    if by > 0:
        return jnp.where(row == 0, 0.0, pltpu.roll(grain, 1, 0))
    return jnp.where(row == GRAIN - 1, 0.0, pltpu.roll(grain, GRAIN - 1, 0))


def half_silu(half):
    return half * jnp.tanh(half) + half


def chain_kernel(
    tm_size,
    space_size,
    rows,
    noise_ref,
    before_ref,
    after_ref,
    far_ref,
    place_ref,
    bias_ref,
    w1a_ref,
    w1b_ref,
    wm_ref,
    w3_ref,
    out_ref,
    state_ref,
    zb_ref,
    first_ref,
    second_ref,
):
    time = place_ref[0]
    tile = place_ref[1]
    top = (tile > 0).astype(F32)
    bottom = (tile < space_size - 1).astype(F32)

    w_new = lax.broadcasted_iota(jnp.int32, (COLS, COLS), 0)
    w_old = lax.broadcasted_iota(jnp.int32, (COLS, COLS), 1)
    order = jnp.where(w_old == (w_new % GRAIN) * 8 + w_new // GRAIN, 1.0, 0.0).astype(BF16)
    lane = lax.broadcasted_iota(jnp.int32, (1, COLS), 1)
    lane_row = lane // 16

    def row_scale(rel):
        if rel < 0:
            return top
        if rel >= rows:
            return bottom
        return None

    def lane_scale(tile_index, halo):
        rel = lane_row + (8 * tile_index - halo)
        return jnp.where(rel < 0, top, jnp.where(rel >= rows, bottom, 1.0))

    total = rows + 2 * HALO
    for t in range(pl.cdiv(total, 8)):
        parts = []
        for e in range(8 * t, 8 * t + 8):
            if e < HALO:
                parts.append(before_ref[e])
            elif e < HALO + rows:
                parts.append(noise_ref[:, e - HALO, :])
            elif e < total:
                parts.append(after_ref[e - HALO - rows])
            else:
                parts.append(jnp.zeros((16, COLS), F32))
        block = jnp.concatenate(parts, axis=0)
        moved = None
        for piece in split3(block):
            part = lax.dot_general(
                order, piece, (((1,), (1,)), ((), ())), preferred_element_type=F32
            )
            moved = part if moved is None else moved + part
        state_ref[t] = moved * lane_scale(t, HALO)

    bias = bias_ref[...]
    params = [far_ref[...], after_ref[HALO], before_ref[HALO]]
    second_ref[...] = jnp.zeros(second_ref.shape, BF16)

    def masked(value, pair, margin):
        halves = []
        scales = [row_scale(2 * pair + i - margin) for i in range(2)]
        if scales[0] is None and scales[1] is None:
            return value
        for i in range(2):
            half = value[:, 128 * i : 128 * (i + 1)]
            halves.append(half if scales[i] is None else half * scales[i])
        return jnp.concatenate(halves, axis=1)

    def keep_first(value, pair, margin):
        value = masked(half_silu(value), pair, margin)
        first_ref[pair, GRAIN : GRAIN + COLS, :] = value.astype(BF16)
        first_ref[pair, 0:GRAIN, :] = shifted_rows(value[COLS - GRAIN :], 1).astype(BF16)
        first_ref[pair, GRAIN + COLS :, :] = shifted_rows(value[:GRAIN], -1).astype(BF16)

    for step in range(ITERS):
        halo = HALO - 3 * step
        count = rows + 2 * halo
        tiles = pl.cdiv(count, 8)
        pairs = (count - 2) // 2
        active = jnp.where(time - ITERS + step >= 0, 1.0, 0.0)
        embed = params[step][0:1] * 0.5
        embed = jnp.concatenate([embed, embed], axis=1)
        keep = params[step][1:2] * active
        rate = params[step][2:3] * active

        for t in range(tiles):
            z = state_ref[t]
            zb_ref[t, GRAIN : GRAIN + COLS, :] = z.astype(BF16)
            zb_ref[t, 0:GRAIN, :] = shifted_rows(z[COLS - GRAIN :], 1).astype(BF16)
            zb_ref[t, GRAIN + COLS :, :] = shifted_rows(z[:GRAIN], -1).astype(BF16)

        def three(t):
            return jnp.concatenate(
                [zb_ref[t, GRAIN * b : GRAIN * b + COLS, :] for b in range(3)], axis=1
            )

        for t in range(tiles):
            here = min(3, pairs - 4 * t)
            if here > 0:
                out = jnp.dot(
                    three(t), w1a_ref[:, : 256 * here], preferred_element_type=F32
                )
                for i in range(here):
                    value = out[:, 256 * i : 256 * (i + 1)] + embed
                    keep_first(value, 4 * t + i, halo - 1)
            if 4 * t + 3 < pairs:
                both = jnp.concatenate([lane < 64] * 3, axis=1)
                out = jnp.dot(
                    jnp.where(both, three(t + 1), three(t)),
                    w1b_ref[...],
                    preferred_element_type=F32,
                )
                keep_first(out + embed, 4 * t + 3, halo - 1)

        chunk = (pairs - 1) // 3
        for start in range(0, pairs - 1, chunk):
            lhs = jnp.concatenate(
                [
                    jnp.concatenate(
                        [
                            first_ref[p + i, GRAIN * b : GRAIN * b + COLS, :]
                            for b in range(3)
                            for i in range(2)
                        ],
                        axis=1,
                    )
                    for p in range(start, start + chunk)
                ],
                axis=0,
            )
            out = jnp.dot(lhs, wm_ref[...], preferred_element_type=F32)
            for i in range(chunk):
                value = masked(
                    half_silu(out[COLS * i : COLS * (i + 1)]), start + i, halo - 2
                )
                second_ref[start + i] = value.astype(BF16)

        new_count = count - 6
        new_tiles = pl.cdiv(new_count, 8)
        lhs = jnp.concatenate(
            [
                jnp.concatenate([second_ref[4 * t + i] for i in range(5)], axis=1)
                for t in range(new_tiles)
            ],
            axis=0,
        )
        out = jnp.dot(lhs, w3_ref[...], preferred_element_type=F32)
        for t in range(new_tiles):
            g = out[COLS * t : COLS * (t + 1)]
            left = g[:, 0:128]
            right = g[:, 256:384]
            left = jnp.concatenate(
                [shifted_rows(left[COLS - GRAIN :], 1), left[: COLS - GRAIN]], axis=0
            )
            right = jnp.concatenate([right[GRAIN:], shifted_rows(right[:GRAIN], -1)], axis=0)
            conv = left + g[:, 128:256] + right
            here = state_ref[t]
            old = jnp.concatenate([here[:, 48:], state_ref[t + 1][:, :48]], axis=1) if (
                t + 1 < tiles
            ) else jnp.concatenate([here[:, 48:], jnp.zeros((COLS, 48), F32)], axis=1)
            new = old + keep * old + rate * (old + conv + bias)
            if step + 1 < ITERS:
                state_ref[t] = new * lane_scale(t, halo - 3)
            else:
                turned = new.T
                moved = None
                for piece in split3(turned):
                    part = jnp.dot(piece, order, preferred_element_type=F32)
                    moved = part if moved is None else moved + part
                for r in range(8):
                    out_ref[0, :, 8 * t + r, :] = moved[16 * r : 16 * r + 16]


def chain(
    start_noise, time_embed, keep_rate, denoise_rate, conv_first, conv_middle, conv_last, out_bias
):
    channels, rows, cols = start_noise.shape
    tm_size = lax.axis_size("tm")
    space_size = lax.axis_size("space")
    vmem = pl.BlockSpec(memory_space=pltpu.VMEM)
    smem = pl.BlockSpec(memory_space=pltpu.SMEM)
    shape = jax.ShapeDtypeStruct

    up, down, far = pl.pallas_call(
        pack_kernel,
        out_shape=(
            pltpu.VMEM((HALO + 1, channels, cols), F32),
            pltpu.VMEM((HALO + 1, channels, cols), F32),
            pltpu.VMEM((8, cols), F32),
        ),
        in_specs=[vmem, vmem, smem, smem],
        out_specs=(vmem, vmem, vmem),
    )(start_noise, time_embed, keep_rate, denoise_rate)

    def moves(times, tiles):
        pairs = []
        for t in range(tm_size):
            for s in range(space_size):
                target = ((t + times) % tm_size) * space_size + (s + tiles) % space_size
                pairs.append((t * space_size + s, target))
        return pairs

    axes = ("tm", "space")
    before = lax.ppermute(up, axes, moves(1, 1))
    after = lax.ppermute(down, axes, moves(2, -1))
    far = lax.ppermute(far, axes, moves(3, 0))

    w1a, w1b, wm, w3, bias = pl.pallas_call(
        weights_kernel,
        out_shape=(
            pltpu.VMEM((384, 768), BF16),
            pltpu.VMEM((384, 256), BF16),
            pltpu.VMEM((1536, 256), BF16),
            pltpu.VMEM((1280, 384), BF16),
            pltpu.VMEM((1, COLS), F32),
        ),
        in_specs=[vmem] * 4,
        out_specs=(vmem,) * 5,
    )(jnp.swapaxes(conv_first, 1, 2), conv_middle, conv_last, out_bias.reshape(1, channels))

    place = jnp.stack([lax.axis_index("tm"), lax.axis_index("space")]).astype(jnp.int32)
    total = rows + 2 * HALO
    pairs = (total - 2) // 2

    def body(*refs):
        chain_kernel(tm_size, space_size, rows, *refs)

    return pl.pallas_call(
        body,
        out_shape=shape((1, channels, rows, cols), F32),
        in_specs=[vmem] * 4 + [smem] + [vmem] * 5,
        out_specs=vmem,
        scratch_shapes=[
            pltpu.VMEM((pl.cdiv(total, 8), COLS, COLS), F32),
            pltpu.VMEM((pl.cdiv(total, 8), PAD, COLS), BF16),
            pltpu.VMEM((pairs, PAD, 256), BF16),
            pltpu.VMEM((pairs + 1, COLS, 256), BF16),
        ],
        compiler_params=pltpu.CompilerParams(vmem_limit_bytes=48 << 20),
    )(start_noise, before, after, far, place, bias, w1a, w1b, wm, w3)


def solution(mesh):
    placed = (
        P(None, ("groups", "space"), None),
        P("tm", None),
        P("tm"),
        P("tm"),
        P(),
        P(),
        P(),
        P(),
    )
    return jax.shard_map(
        chain if mesh.shape["tm"] == ITERS + 1 else picard,
        mesh=mesh,
        in_specs=placed,
        out_specs=P("tm", None, ("groups", "space"), None),
        check_vma=False,
    )
```

```python
import jax
import jax.numpy as jnp
from jax import lax
from jax.experimental import pallas as pl
from jax.experimental.pallas import tpu as pltpu
from jax.sharding import PartitionSpec as P

ITERS = 3
HALO = 3 * ITERS
BF16 = jnp.bfloat16
F32 = jnp.float32


def padded(value, sides, width):
    for axis, dim in sides:
        count, length = (lax.axis_size(axis), value.shape[dim])
        up = [(i, (i + 1) % count) for i in range(count - 1)]
        down = [(j, i) for i, j in up]
        last = lax.slice_in_dim(value, length - width, length, axis=dim)
        initial = lax.slice_in_dim(value, 0, width, axis=dim)
        before = lax.ppermute(last, axis, up)
        after = lax.ppermute(initial, axis, down)
        value = jnp.concatenate([before, value, after], axis=dim)
    return value


def carried_in(part, axis):
    place = lax.axis_index(axis)
    gathered = lax.all_gather(part, axis)
    earlier = jnp.arange(gathered.shape[0]) < place
    return jnp.sum(jnp.where(earlier[:, None, None, None], gathered, 0.0), axis=0)


def convolve(field, taps):
    kernel = taps.reshape((3, 3, taps.shape[1], taps.shape[2]))
    result = lax.conv_general_dilated(
        field[None],
        kernel,
        (1, 1),
        ((0, 0), (1, 1)),
        dimension_numbers=("NCHW", "HWOI", "NCHW"),
        preferred_element_type=F32,
    )
    return result[0]


def inside_rows(margin, count, tile_rows):
    glob_row = lax.axis_index("space") * tile_rows - margin + jnp.arange(count, dtype=jnp.int32)
    valid = (glob_row >= 0) & (glob_row < tile_rows * lax.axis_size("space"))
    return valid.astype(F32)[None, :, None]


def picard(
    start_noise, time_embed, keep_rate, denoise_rate, conv_first, conv_middle, conv_last, out_bias
):
    tile_rows = start_noise.shape[1]
    embed = time_embed[0][:, None, None]
    keep = keep_rate[0]
    rate = denoise_rate[0]
    bias = out_bias[:, None, None]
    state = start_noise
    for step in range(ITERS):
        inputs = state.astype(BF16)
        extended = padded(inputs, (("space", 1),), 3)
        first = jax.nn.silu(convolve(extended, conv_first) + embed)
        first = (first * inside_rows(2, tile_rows + 4, tile_rows)).astype(BF16)
        second = jax.nn.silu(convolve(first, conv_middle))
        second = (second * inside_rows(1, tile_rows + 2, tile_rows)).astype(BF16)
        last = convolve(second, conv_last)
        denoised = state + last + bias
        drift = keep * state + rate * denoised
        state = start_noise + carried_in(drift, "tm")
    return state[None]


COLS = 128
GRAIN = 16
PAD = COLS + 2 * GRAIN


def pack_kernel(noise_ref, embed_ref, keep_ref, rate_ref, up_ref, down_ref, far_ref):
    rows = noise_ref.shape[1]
    params = jnp.concatenate(
        [
            embed_ref[...],
            jnp.full((1, COLS), keep_ref[0], F32),
            jnp.full((1, COLS), rate_ref[0], F32),
            jnp.zeros((5, COLS), F32),
        ],
        axis=0,
    )
    full = jnp.concatenate([params, jnp.zeros((8, COLS), F32)], axis=0)
    for i in range(HALO):
        up_ref[i] = noise_ref[:, rows - HALO + i, :]
        down_ref[i] = noise_ref[:, i, :]
    up_ref[HALO] = full
    down_ref[HALO] = full
    far_ref[...] = params


def weights_kernel(
    first_ref, middle_ref, last_ref, bias_in_ref, w1a_ref, w1b_ref, wm_ref, w3_ref, bias_ref
):
    bias_ref[...] = jnp.concatenate([bias_in_ref[...]] * 8, axis=1)
    w1a_ref[...] = jnp.zeros(w1a_ref.shape, BF16)
    w1b_ref[...] = jnp.zeros(w1b_ref.shape, BF16)
    for tap in range(9):
        a, b = divmod(tap, 3)
        block = first_ref[tap] * BF16(0.5)
        for out in range(6):
            row = out + a
            w1a_ref[pl.ds(128 * b + 16 * row, 16), pl.ds(128 * out, 128)] = block
        for out in range(2):
            row = 6 + out + a
            place = row - 8 if row >= 8 else row
            w1b_ref[pl.ds(128 * b + 16 * place, 16), pl.ds(128 * out, 128)] = block
        block = (middle_ref[tap].astype(F32).T * 0.5).astype(BF16)
        for out in range(2):
            wm_ref[pl.ds(512 * b + 128 * (out + a), 128), pl.ds(128 * out, 128)] = block
    zero = jnp.zeros((128, 128), BF16)
    for b in range(3):
        wm_ref[pl.ds(512 * b + 384, 128), pl.ds(0, 128)] = zero
        wm_ref[pl.ds(512 * b, 128), pl.ds(128, 128)] = zero
        for row in range(10):
            parts = []
            for out in range(8):
                a = row - out
                if 0 <= a < 3:
                    parts.append(last_ref[3 * a + b].astype(F32))
                else:
                    parts.append(jnp.zeros((16, 128), F32))
            block = jnp.concatenate(parts, axis=0).T.astype(BF16)
            w3_ref[pl.ds(128 * row, 128), pl.ds(128 * b, 128)] = block


def split3(value):
    high = value.astype(BF16)
    rest = value - high.astype(F32)
    mid = rest.astype(BF16)
    low = (rest - mid.astype(F32)).astype(BF16)
    return high, mid, low


def shifted_rows(grain, by):
    row = lax.broadcasted_iota(jnp.int32, grain.shape, 0)
    if by > 0:
        return jnp.where(row == 0, 0.0, pltpu.roll(grain, 1, 0))
    return jnp.where(row == GRAIN - 1, 0.0, pltpu.roll(grain, GRAIN - 1, 0))


def half_silu(half):
    return half * jnp.tanh(half) + half


def chain_kernel(
    tm_size,
    space_size,
    rows,
    noise_ref,
    before_ref,
    after_ref,
    far_ref,
    place_ref,
    bias_ref,
    w1a_ref,
    w1b_ref,
    wm_ref,
    w3_ref,
    out_ref,
    state_ref,
    zb_ref,
    first_ref,
    second_ref,
):
    time = place_ref[0]
    tile = place_ref[1]
    top = (tile > 0).astype(F32)
    bottom = (tile < space_size - 1).astype(F32)

    w_new = lax.broadcasted_iota(jnp.int32, (COLS, COLS), 0)
    w_old = lax.broadcasted_iota(jnp.int32, (COLS, COLS), 1)
    order = jnp.where(w_old == (w_new % GRAIN) * 8 + w_new // GRAIN, 1.0, 0.0).astype(BF16)
    lane = lax.broadcasted_iota(jnp.int32, (1, COLS), 1)
    lane_row = lane // 16

    def row_scale(rel):
        if rel < 0:
            return top
        if rel >= rows:
            return bottom
        return None

    def lane_scale(tile_index, halo):
        rel = lane_row + (8 * tile_index - halo)
        return jnp.where(rel < 0, top, jnp.where(rel >= rows, bottom, 1.0))

    def build_state(halo):
        total = rows + 2 * halo
        for t in range(pl.cdiv(total, 8)):
            parts = []
            for e in range(8 * t, 8 * t + 8):
                if e < halo:
                    parts.append(before_ref[HALO - halo + e])
                elif e < halo + rows:
                    parts.append(noise_ref[:, e - halo, :])
                elif e < total:
                    parts.append(after_ref[e - halo - rows])
                else:
                    parts.append(jnp.zeros((16, COLS), F32))
            block = jnp.concatenate(parts, axis=0)
            moved = None
            for piece in split3(block):
                part = lax.dot_general(
                    order, piece, (((1,), (1,)), ((), ())), preferred_element_type=F32
                )
                moved = part if moved is None else moved + part
            state_ref[t] = moved * lane_scale(t, halo)

    bias = bias_ref[...]
    params = [far_ref[...], after_ref[HALO], before_ref[HALO]]

    def masked(value, pair, margin):
        halves = []
        scales = [row_scale(2 * pair + i - margin) for i in range(2)]
        if scales[0] is None and scales[1] is None:
            return value
        for i in range(2):
            half = value[:, 128 * i : 128 * (i + 1)]
            halves.append(half if scales[i] is None else half * scales[i])
        return jnp.concatenate(halves, axis=1)

    def keep_first(value, pair, margin):
        value = masked(half_silu(value), pair, margin)
        first_ref[pair, GRAIN : GRAIN + COLS, :] = value.astype(BF16)
        first_ref[pair, 0:GRAIN, :] = shifted_rows(value[COLS - GRAIN :], 1).astype(BF16)
        first_ref[pair, GRAIN + COLS :, :] = shifted_rows(value[:GRAIN], -1).astype(BF16)

    def one_step(step):
        halo = HALO - 3 * step
        count = rows + 2 * halo
        tiles = pl.cdiv(count, 8)
        pairs = (count - 2) // 2
        embed = params[step][0:1] * 0.5
        embed = jnp.concatenate([embed, embed], axis=1)
        keep = params[step][1:2]
        rate = params[step][2:3]

        for t in range(tiles):
            z = state_ref[t]
            zb_ref[t, GRAIN : GRAIN + COLS, :] = z.astype(BF16)
            zb_ref[t, 0:GRAIN, :] = shifted_rows(z[COLS - GRAIN :], 1).astype(BF16)
            zb_ref[t, GRAIN + COLS :, :] = shifted_rows(z[:GRAIN], -1).astype(BF16)

        def three(t):
            return jnp.concatenate(
                [zb_ref[t, GRAIN * b : GRAIN * b + COLS, :] for b in range(3)], axis=1
            )

        for t in range(tiles):
            here = min(3, pairs - 4 * t)
            if here > 0:
                out = jnp.dot(
                    three(t), w1a_ref[:, : 256 * here], preferred_element_type=F32
                )
                for i in range(here):
                    value = out[:, 256 * i : 256 * (i + 1)] + embed
                    keep_first(value, 4 * t + i, halo - 1)
            if 4 * t + 3 < pairs:
                both = jnp.concatenate([lane < 64] * 3, axis=1)
                out = jnp.dot(
                    jnp.where(both, three(t + 1), three(t)),
                    w1b_ref[...],
                    preferred_element_type=F32,
                )
                keep_first(out + embed, 4 * t + 3, halo - 1)

        chunk = (pairs - 1) // 3
        for start in range(0, pairs - 1, chunk):
            lhs = jnp.concatenate(
                [
                    jnp.concatenate(
                        [
                            first_ref[p + i, GRAIN * b : GRAIN * b + COLS, :]
                            for b in range(3)
                            for i in range(2)
                        ],
                        axis=1,
                    )
                    for p in range(start, start + chunk)
                ],
                axis=0,
            )
            out = jnp.dot(lhs, wm_ref[...], preferred_element_type=F32)
            for i in range(chunk):
                value = masked(
                    half_silu(out[COLS * i : COLS * (i + 1)]), start + i, halo - 2
                )
                second_ref[start + i] = value.astype(BF16)

        new_count = count - 6
        new_tiles = pl.cdiv(new_count, 8)
        for i in range(pairs - 1, 4 * new_tiles + 1):
            second_ref[i] = jnp.zeros((COLS, 256), BF16)
        lhs = jnp.concatenate(
            [
                jnp.concatenate([second_ref[4 * t + i] for i in range(5)], axis=1)
                for t in range(new_tiles)
            ],
            axis=0,
        )
        out = jnp.dot(lhs, w3_ref[...], preferred_element_type=F32)
        for t in range(new_tiles):
            g = out[COLS * t : COLS * (t + 1)]
            left = g[:, 0:128]
            right = g[:, 256:384]
            left = jnp.concatenate(
                [shifted_rows(left[COLS - GRAIN :], 1), left[: COLS - GRAIN]], axis=0
            )
            right = jnp.concatenate([right[GRAIN:], shifted_rows(right[:GRAIN], -1)], axis=0)
            conv = left + g[:, 128:256] + right
            here = state_ref[t]
            old = jnp.concatenate([here[:, 48:], state_ref[t + 1][:, :48]], axis=1) if (
                t + 1 < tiles
            ) else jnp.concatenate([here[:, 48:], jnp.zeros((COLS, 48), F32)], axis=1)
            new = old + keep * old + rate * (old + conv + bias)
            if step + 1 < ITERS:
                state_ref[t] = new * lane_scale(t, halo - 3)
            else:
                turned = new.T
                moved = None
                for piece in split3(turned):
                    part = jnp.dot(piece, order, preferred_element_type=F32)
                    moved = part if moved is None else moved + part
                for r in range(8):
                    out_ref[0, :, 8 * t + r, :] = moved[16 * r : 16 * r + 16]

    for step in range(ITERS):

        @pl.when(time == ITERS - step)
        def _():
            build_state(HALO - 3 * step)

        @pl.when(time >= ITERS - step)
        def _():
            one_step(step)

    @pl.when(time == 0)
    def _():
        out_ref[0] = noise_ref[...]


def chain(
    start_noise, time_embed, keep_rate, denoise_rate, conv_first, conv_middle, conv_last, out_bias
):
    channels, rows, cols = start_noise.shape
    tm_size = lax.axis_size("tm")
    space_size = lax.axis_size("space")
    vmem = pl.BlockSpec(memory_space=pltpu.VMEM)
    smem = pl.BlockSpec(memory_space=pltpu.SMEM)
    shape = jax.ShapeDtypeStruct

    up, down, far = pl.pallas_call(
        pack_kernel,
        out_shape=(
            pltpu.VMEM((HALO + 1, channels, cols), F32),
            pltpu.VMEM((HALO + 1, channels, cols), F32),
            pltpu.VMEM((8, cols), F32),
        ),
        in_specs=[vmem, vmem, smem, smem],
        out_specs=(vmem, vmem, vmem),
    )(start_noise, time_embed, keep_rate, denoise_rate)

    def moves(times, tiles):
        return [
            (t * space_size + s, u * space_size + (s + tiles) % space_size)
            for t, u in times
            for s in range(space_size)
        ]

    axes = ("tm", "space")
    before = lax.ppermute(up, axes, moves([(0, 1), (1, 2), (2, 3)], 1))
    after = lax.ppermute(down, axes, moves([(0, 2), (1, 3), (2, 1)], -1))
    far = lax.ppermute(far, axes, moves([(0, 3)], 0))

    w1a, w1b, wm, w3, bias = pl.pallas_call(
        weights_kernel,
        out_shape=(
            pltpu.VMEM((384, 768), BF16),
            pltpu.VMEM((384, 256), BF16),
            pltpu.VMEM((1536, 256), BF16),
            pltpu.VMEM((1280, 384), BF16),
            pltpu.VMEM((1, COLS), F32),
        ),
        in_specs=[vmem] * 4,
        out_specs=(vmem,) * 5,
    )(jnp.swapaxes(conv_first, 1, 2), conv_middle, conv_last, out_bias.reshape(1, channels))

    place = jnp.stack([lax.axis_index("tm"), lax.axis_index("space")]).astype(jnp.int32)
    total = rows + 2 * HALO
    pairs = (total - 2) // 2

    def body(*refs):
        chain_kernel(tm_size, space_size, rows, *refs)

    return pl.pallas_call(
        body,
        out_shape=shape((1, channels, rows, cols), F32),
        in_specs=[vmem] * 4 + [smem] + [vmem] * 5,
        out_specs=vmem,
        scratch_shapes=[
            pltpu.VMEM((pl.cdiv(total, 8), COLS, COLS), F32),
            pltpu.VMEM((pl.cdiv(total, 8), PAD, COLS), BF16),
            pltpu.VMEM((pairs, PAD, 256), BF16),
            pltpu.VMEM((pairs + 1, COLS, 256), BF16),
        ],
        compiler_params=pltpu.CompilerParams(vmem_limit_bytes=48 << 20),
    )(start_noise, before, after, far, place, bias, w1a, w1b, wm, w3)


def solution(mesh):
    placed = (
        P(None, ("groups", "space"), None),
        P("tm", None),
        P("tm"),
        P("tm"),
        P(),
        P(),
        P(),
        P(),
    )
    return jax.shard_map(
        chain if mesh.shape["tm"] == ITERS + 1 else picard,
        mesh=mesh,
        in_specs=placed,
        out_specs=P("tm", None, ("groups", "space"), None),
        check_vma=False,
    )
```

```python
import jax
import jax.numpy as jnp
from jax import lax
from jax.experimental import pallas as pl
from jax.experimental.pallas import tpu as pltpu
from jax.sharding import PartitionSpec as P

ITERS = 3
HALO = 3 * ITERS
BF16 = jnp.bfloat16
F32 = jnp.float32


def padded(value, sides, width):
    for axis, dim in sides:
        count, length = (lax.axis_size(axis), value.shape[dim])
        up = [(i, (i + 1) % count) for i in range(count - 1)]
        down = [(j, i) for i, j in up]
        last = lax.slice_in_dim(value, length - width, length, axis=dim)
        initial = lax.slice_in_dim(value, 0, width, axis=dim)
        before = lax.ppermute(last, axis, up)
        after = lax.ppermute(initial, axis, down)
        value = jnp.concatenate([before, value, after], axis=dim)
    return value


def carried_in(part, axis):
    place = lax.axis_index(axis)
    gathered = lax.all_gather(part, axis)
    earlier = jnp.arange(gathered.shape[0]) < place
    return jnp.sum(jnp.where(earlier[:, None, None, None], gathered, 0.0), axis=0)


def convolve(field, taps):
    kernel = taps.reshape((3, 3, taps.shape[1], taps.shape[2]))
    result = lax.conv_general_dilated(
        field[None],
        kernel,
        (1, 1),
        ((0, 0), (1, 1)),
        dimension_numbers=("NCHW", "HWOI", "NCHW"),
        preferred_element_type=F32,
    )
    return result[0]


def inside_rows(margin, count, tile_rows):
    glob_row = lax.axis_index("space") * tile_rows - margin + jnp.arange(count, dtype=jnp.int32)
    valid = (glob_row >= 0) & (glob_row < tile_rows * lax.axis_size("space"))
    return valid.astype(F32)[None, :, None]


def picard(
    start_noise, time_embed, keep_rate, denoise_rate, conv_first, conv_middle, conv_last, out_bias
):
    tile_rows = start_noise.shape[1]
    embed = time_embed[0][:, None, None]
    keep = keep_rate[0]
    rate = denoise_rate[0]
    bias = out_bias[:, None, None]
    state = start_noise
    for step in range(ITERS):
        inputs = state.astype(BF16)
        extended = padded(inputs, (("space", 1),), 3)
        first = jax.nn.silu(convolve(extended, conv_first) + embed)
        first = (first * inside_rows(2, tile_rows + 4, tile_rows)).astype(BF16)
        second = jax.nn.silu(convolve(first, conv_middle))
        second = (second * inside_rows(1, tile_rows + 2, tile_rows)).astype(BF16)
        last = convolve(second, conv_last)
        denoised = state + last + bias
        drift = keep * state + rate * denoised
        state = start_noise + carried_in(drift, "tm")
    return state[None]


COLS = 128
GRAIN = 16
PAD = COLS + 2 * GRAIN


def weights_kernel(
    first_ref, middle_ref, last_ref, bias_in_ref, w1a_ref, w1b_ref, wm_ref, w3_ref, bias_ref
):
    bias_ref[...] = jnp.concatenate([bias_in_ref[...]] * 8, axis=1)
    w1a_ref[...] = jnp.zeros(w1a_ref.shape, BF16)
    w1b_ref[...] = jnp.zeros(w1b_ref.shape, BF16)
    for tap in range(9):
        a, b = divmod(tap, 3)
        block = first_ref[tap] * BF16(0.5)
        for out in range(6):
            row = out + a
            w1a_ref[pl.ds(128 * b + 16 * row, 16), pl.ds(128 * out, 128)] = block
        for out in range(2):
            row = 6 + out + a
            place = row - 8 if row >= 8 else row
            w1b_ref[pl.ds(128 * b + 16 * place, 16), pl.ds(128 * out, 128)] = block
        block = (middle_ref[tap].astype(F32).T * 0.5).astype(BF16)
        for out in range(2):
            wm_ref[pl.ds(512 * b + 128 * (out + a), 128), pl.ds(128 * out, 128)] = block
    zero = jnp.zeros((128, 128), BF16)
    for b in range(3):
        wm_ref[pl.ds(512 * b + 384, 128), pl.ds(0, 128)] = zero
        wm_ref[pl.ds(512 * b, 128), pl.ds(128, 128)] = zero
        for row in range(10):
            parts = []
            for out in range(8):
                a = row - out
                if 0 <= a < 3:
                    parts.append(last_ref[3 * a + b].astype(F32))
                else:
                    parts.append(jnp.zeros((16, 128), F32))
            block = jnp.concatenate(parts, axis=0).T.astype(BF16)
            w3_ref[pl.ds(128 * row, 128), pl.ds(128 * b, 128)] = block


def split3(value):
    high = value.astype(BF16)
    rest = value - high.astype(F32)
    mid = rest.astype(BF16)
    low = (rest - mid.astype(F32)).astype(BF16)
    return high, mid, low


def shifted_rows(grain, by):
    row = lax.broadcasted_iota(jnp.int32, grain.shape, 0)
    if by > 0:
        return jnp.where(row == 0, 0.0, pltpu.roll(grain, 1, 0))
    return jnp.where(row == GRAIN - 1, 0.0, pltpu.roll(grain, GRAIN - 1, 0))


def half_silu(half):
    return half * jnp.tanh(half) + half


def chain_kernel(
    tm_size,
    space_size,
    rows,
    noise_ref,
    before_ref,
    after_ref,
    one_ref,
    two_ref,
    three_ref,
    place_ref,
    bias_ref,
    w1a_ref,
    w1b_ref,
    wm_ref,
    w3_ref,
    out_ref,
    state_ref,
    zb_ref,
    first_ref,
    second_ref,
):
    time = place_ref[0]
    tile = place_ref[1]
    top = (tile > 0).astype(F32)
    bottom = (tile < space_size - 1).astype(F32)

    w_new = lax.broadcasted_iota(jnp.int32, (COLS, COLS), 0)
    w_old = lax.broadcasted_iota(jnp.int32, (COLS, COLS), 1)
    order = jnp.where(w_old == (w_new % GRAIN) * 8 + w_new // GRAIN, 1.0, 0.0).astype(BF16)
    lane = lax.broadcasted_iota(jnp.int32, (1, COLS), 1)
    lane_row = lane // 16

    def row_scale(rel):
        if rel < 0:
            return top
        if rel >= rows:
            return bottom
        return None

    def lane_scale(tile_index, halo):
        rel = lane_row + (8 * tile_index - halo)
        return jnp.where(rel < 0, top, jnp.where(rel >= rows, bottom, 1.0))

    def build_state(halo):
        total = rows + 2 * halo
        for t in range(pl.cdiv(total, 8)):
            parts = []
            for e in range(8 * t, 8 * t + 8):
                if e < halo:
                    parts.append(before_ref[:, rows - halo + e, :])
                elif e < halo + rows:
                    parts.append(noise_ref[:, e - halo, :])
                elif e < total:
                    parts.append(after_ref[:, e - halo - rows, :])
                else:
                    parts.append(jnp.zeros((16, COLS), F32))
            block = jnp.concatenate(parts, axis=0)
            moved = None
            for piece in split3(block):
                part = lax.dot_general(
                    order, piece, (((1,), (1,)), ((), ())), preferred_element_type=F32
                )
                moved = part if moved is None else moved + part
            state_ref[t] = moved * lane_scale(t, halo)

    bias = bias_ref[...]
    params = [two_ref[3:6], two_ref[0:3], one_ref[...]]

    def masked(value, pair, margin):
        halves = []
        scales = [row_scale(2 * pair + i - margin) for i in range(2)]
        if scales[0] is None and scales[1] is None:
            return value
        for i in range(2):
            half = value[:, 128 * i : 128 * (i + 1)]
            halves.append(half if scales[i] is None else half * scales[i])
        return jnp.concatenate(halves, axis=1)

    def keep_first(value, pair, margin):
        value = masked(half_silu(value), pair, margin)
        first_ref[pair, GRAIN : GRAIN + COLS, :] = value.astype(BF16)
        first_ref[pair, 0:GRAIN, :] = shifted_rows(value[COLS - GRAIN :], 1).astype(BF16)
        first_ref[pair, GRAIN + COLS :, :] = shifted_rows(value[:GRAIN], -1).astype(BF16)

    def one_step(step):
        halo = HALO - 3 * step
        count = rows + 2 * halo
        tiles = pl.cdiv(count, 8)
        pairs = (count - 2) // 2
        embed = params[step][0:1] * 0.5
        embed = jnp.concatenate([embed, embed], axis=1)
        keep = params[step][1:2]
        rate = params[step][2:3]

        for t in range(tiles):
            z = state_ref[t]
            zb_ref[t, GRAIN : GRAIN + COLS, :] = z.astype(BF16)
            zb_ref[t, 0:GRAIN, :] = shifted_rows(z[COLS - GRAIN :], 1).astype(BF16)
            zb_ref[t, GRAIN + COLS :, :] = shifted_rows(z[:GRAIN], -1).astype(BF16)

        def three(t):
            return jnp.concatenate(
                [zb_ref[t, GRAIN * b : GRAIN * b + COLS, :] for b in range(3)], axis=1
            )

        for t in range(tiles):
            here = min(3, pairs - 4 * t)
            if here > 0:
                out = jnp.dot(
                    three(t), w1a_ref[:, : 256 * here], preferred_element_type=F32
                )
                for i in range(here):
                    value = out[:, 256 * i : 256 * (i + 1)] + embed
                    keep_first(value, 4 * t + i, halo - 1)
            if 4 * t + 3 < pairs:
                both = jnp.concatenate([lane < 64] * 3, axis=1)
                out = jnp.dot(
                    jnp.where(both, three(t + 1), three(t)),
                    w1b_ref[...],
                    preferred_element_type=F32,
                )
                keep_first(out + embed, 4 * t + 3, halo - 1)

        chunk = (pairs - 1) // 3
        for start in range(0, pairs - 1, chunk):
            lhs = jnp.concatenate(
                [
                    jnp.concatenate(
                        [
                            first_ref[p + i, GRAIN * b : GRAIN * b + COLS, :]
                            for b in range(3)
                            for i in range(2)
                        ],
                        axis=1,
                    )
                    for p in range(start, start + chunk)
                ],
                axis=0,
            )
            out = jnp.dot(lhs, wm_ref[...], preferred_element_type=F32)
            for i in range(chunk):
                value = masked(
                    half_silu(out[COLS * i : COLS * (i + 1)]), start + i, halo - 2
                )
                second_ref[start + i] = value.astype(BF16)

        new_count = count - 6
        new_tiles = pl.cdiv(new_count, 8)
        for i in range(pairs - 1, 4 * new_tiles + 1):
            second_ref[i] = jnp.zeros((COLS, 256), BF16)
        lhs = jnp.concatenate(
            [
                jnp.concatenate([second_ref[4 * t + i] for i in range(5)], axis=1)
                for t in range(new_tiles)
            ],
            axis=0,
        )
        out = jnp.dot(lhs, w3_ref[...], preferred_element_type=F32)
        for t in range(new_tiles):
            g = out[COLS * t : COLS * (t + 1)]
            left = g[:, 0:128]
            right = g[:, 256:384]
            left = jnp.concatenate(
                [shifted_rows(left[COLS - GRAIN :], 1), left[: COLS - GRAIN]], axis=0
            )
            right = jnp.concatenate([right[GRAIN:], shifted_rows(right[:GRAIN], -1)], axis=0)
            conv = left + g[:, 128:256] + right
            here = state_ref[t]
            old = jnp.concatenate([here[:, 48:], state_ref[t + 1][:, :48]], axis=1) if (
                t + 1 < tiles
            ) else jnp.concatenate([here[:, 48:], jnp.zeros((COLS, 48), F32)], axis=1)
            new = old + keep * old + rate * (old + conv + bias)
            if step + 1 < ITERS:
                state_ref[t] = new * lane_scale(t, halo - 3)
            else:
                turned = new.T
                moved = None
                for piece in split3(turned):
                    part = jnp.dot(piece, order, preferred_element_type=F32)
                    moved = part if moved is None else moved + part
                for r in range(8):
                    out_ref[0, :, 8 * t + r, :] = moved[16 * r : 16 * r + 16]

    for step in range(ITERS):

        @pl.when(time == ITERS - step)
        def _():
            build_state(HALO - 3 * step)

        @pl.when(time >= ITERS - step)
        def _():
            one_step(step)

    @pl.when(time == 0)
    def _():
        out_ref[0] = noise_ref[...]


def chain(
    start_noise, time_embed, keep_rate, denoise_rate, conv_first, conv_middle, conv_last, out_bias
):
    channels, rows, cols = start_noise.shape
    tm_size = lax.axis_size("tm")
    space_size = lax.axis_size("space")
    vmem = pl.BlockSpec(memory_space=pltpu.VMEM)
    smem = pl.BlockSpec(memory_space=pltpu.SMEM)
    shape = jax.ShapeDtypeStruct

    far = jnp.concatenate(
        [
            time_embed,
            jnp.broadcast_to(keep_rate[:, None], (1, cols)),
            jnp.broadcast_to(denoise_rate[:, None], (1, cols)),
        ],
        axis=0,
    )

    def moves(times, tiles):
        return [
            (t * space_size + s, u * space_size + (s + tiles) % space_size)
            for t, u in times
            for s in range(space_size)
        ]

    axes = ("tm", "space")
    own = [(t, t) for t in range(tm_size)]
    before = lax.ppermute(start_noise, axes, moves(own, 1))
    after = lax.ppermute(start_noise, axes, moves(own, -1))
    one = lax.ppermute(far, "tm", [(0, 1), (1, 2), (2, 3), (3, 0)])
    both = jnp.concatenate([far, one], axis=0)
    two = lax.ppermute(both, "tm", [(0, 2), (1, 3), (2, 0), (3, 1)])
    three = one

    w1a, w1b, wm, w3, bias = pl.pallas_call(
        weights_kernel,
        out_shape=(
            pltpu.VMEM((384, 768), BF16),
            pltpu.VMEM((384, 256), BF16),
            pltpu.VMEM((1536, 256), BF16),
            pltpu.VMEM((1280, 384), BF16),
            pltpu.VMEM((1, COLS), F32),
        ),
        in_specs=[vmem] * 4,
        out_specs=(vmem,) * 5,
    )(jnp.swapaxes(conv_first, 1, 2), conv_middle, conv_last, out_bias.reshape(1, channels))

    place = jnp.stack([lax.axis_index("tm"), lax.axis_index("space")]).astype(jnp.int32)
    total = rows + 2 * HALO
    pairs = (total - 2) // 2

    def body(*refs):
        chain_kernel(tm_size, space_size, rows, *refs)

    return pl.pallas_call(
        body,
        out_shape=shape((1, channels, rows, cols), F32),
        in_specs=[vmem] * 6 + [smem] + [vmem] * 5,
        out_specs=vmem,
        scratch_shapes=[
            pltpu.VMEM((pl.cdiv(total, 8), COLS, COLS), F32),
            pltpu.VMEM((pl.cdiv(total, 8), PAD, COLS), BF16),
            pltpu.VMEM((pairs, PAD, 256), BF16),
            pltpu.VMEM((pairs + 1, COLS, 256), BF16),
        ],
        compiler_params=pltpu.CompilerParams(vmem_limit_bytes=48 << 20),
    )(start_noise, before, after, one, two, three, place, bias, w1a, w1b, wm, w3)


def solution(mesh):
    placed = (
        P(None, ("groups", "space"), None),
        P("tm", None),
        P("tm"),
        P("tm"),
        P(),
        P(),
        P(),
        P(),
    )
    return jax.shard_map(
        chain if mesh.shape["tm"] == ITERS + 1 else picard,
        mesh=mesh,
        in_specs=placed,
        out_specs=P("tm", None, ("groups", "space"), None),
        check_vma=False,
    )
```

```python
import jax
import jax.numpy as jnp
from jax import lax
from jax.experimental import pallas as pl
from jax.experimental.pallas import tpu as pltpu
from jax.sharding import PartitionSpec as P

ITERS = 3
HALO = 3 * ITERS
BF16 = jnp.bfloat16
F32 = jnp.float32


def padded(value, sides, width):
    for axis, dim in sides:
        count, length = (lax.axis_size(axis), value.shape[dim])
        up = [(i, (i + 1) % count) for i in range(count - 1)]
        down = [(j, i) for i, j in up]
        last = lax.slice_in_dim(value, length - width, length, axis=dim)
        initial = lax.slice_in_dim(value, 0, width, axis=dim)
        before = lax.ppermute(last, axis, up)
        after = lax.ppermute(initial, axis, down)
        value = jnp.concatenate([before, value, after], axis=dim)
    return value


def carried_in(part, axis):
    place = lax.axis_index(axis)
    gathered = lax.all_gather(part, axis)
    earlier = jnp.arange(gathered.shape[0]) < place
    return jnp.sum(jnp.where(earlier[:, None, None, None], gathered, 0.0), axis=0)


def convolve(field, taps):
    kernel = taps.reshape((3, 3, taps.shape[1], taps.shape[2]))
    result = lax.conv_general_dilated(
        field[None],
        kernel,
        (1, 1),
        ((0, 0), (1, 1)),
        dimension_numbers=("NCHW", "HWOI", "NCHW"),
        preferred_element_type=F32,
    )
    return result[0]


def inside_rows(margin, count, tile_rows):
    glob_row = lax.axis_index("space") * tile_rows - margin + jnp.arange(count, dtype=jnp.int32)
    valid = (glob_row >= 0) & (glob_row < tile_rows * lax.axis_size("space"))
    return valid.astype(F32)[None, :, None]


def picard(
    start_noise, time_embed, keep_rate, denoise_rate, conv_first, conv_middle, conv_last, out_bias
):
    tile_rows = start_noise.shape[1]
    embed = time_embed[0][:, None, None]
    keep = keep_rate[0]
    rate = denoise_rate[0]
    bias = out_bias[:, None, None]
    state = start_noise
    for step in range(ITERS):
        inputs = state.astype(BF16)
        extended = padded(inputs, (("space", 1),), 3)
        first = jax.nn.silu(convolve(extended, conv_first) + embed)
        first = (first * inside_rows(2, tile_rows + 4, tile_rows)).astype(BF16)
        second = jax.nn.silu(convolve(first, conv_middle))
        second = (second * inside_rows(1, tile_rows + 2, tile_rows)).astype(BF16)
        last = convolve(second, conv_last)
        denoised = state + last + bias
        drift = keep * state + rate * denoised
        state = start_noise + carried_in(drift, "tm")
    return state[None]


COLS = 128
GRAIN = 16
PAD = COLS + 2 * GRAIN


def weights_kernel(
    first_ref, middle_ref, last_ref, bias_in_ref, w1a_ref, w1b_ref, wm_ref, w3_ref, bias_ref
):
    bias_ref[...] = jnp.concatenate([bias_in_ref[...]] * 8, axis=1)
    w1a_ref[...] = jnp.zeros(w1a_ref.shape, BF16)
    w1b_ref[...] = jnp.zeros(w1b_ref.shape, BF16)
    for tap in range(9):
        a, b = divmod(tap, 3)
        block = first_ref[tap] * BF16(0.5)
        for out in range(6):
            row = out + a
            w1a_ref[pl.ds(128 * b + 16 * row, 16), pl.ds(128 * out, 128)] = block
        for out in range(2):
            row = 6 + out + a
            place = row - 8 if row >= 8 else row
            w1b_ref[pl.ds(128 * b + 16 * place, 16), pl.ds(128 * out, 128)] = block
        block = (middle_ref[tap].astype(F32).T * 0.5).astype(BF16)
        for out in range(2):
            wm_ref[pl.ds(512 * b + 128 * (out + a), 128), pl.ds(128 * out, 128)] = block
    zero = jnp.zeros((128, 128), BF16)
    for b in range(3):
        wm_ref[pl.ds(512 * b + 384, 128), pl.ds(0, 128)] = zero
        wm_ref[pl.ds(512 * b, 128), pl.ds(128, 128)] = zero
        for row in range(10):
            parts = []
            for out in range(8):
                a = row - out
                if 0 <= a < 3:
                    parts.append(last_ref[3 * a + b].astype(F32))
                else:
                    parts.append(jnp.zeros((16, 128), F32))
            block = jnp.concatenate(parts, axis=0).T.astype(BF16)
            w3_ref[pl.ds(128 * row, 128), pl.ds(128 * b, 128)] = block


def split3(value):
    high = value.astype(BF16)
    rest = value - high.astype(F32)
    mid = rest.astype(BF16)
    low = (rest - mid.astype(F32)).astype(BF16)
    return high, mid, low


def shifted_rows(grain, by):
    row = lax.broadcasted_iota(jnp.int32, grain.shape, 0)
    if by > 0:
        return jnp.where(row == 0, 0.0, pltpu.roll(grain, 1, 0))
    return jnp.where(row == GRAIN - 1, 0.0, pltpu.roll(grain, GRAIN - 1, 0))


def half_silu(half):
    return half * jnp.tanh(half) + half


def chain_kernel(
    tm_size,
    space_size,
    rows,
    noise_ref,
    before_ref,
    after_ref,
    one_ref,
    two_ref,
    three_ref,
    place_ref,
    bias_ref,
    w1a_ref,
    w1b_ref,
    wm_ref,
    w3_ref,
    out_ref,
    state_ref,
    zb_ref,
    first_ref,
    second_ref,
):
    time = place_ref[0]
    tile = place_ref[1]
    top = (tile > 0).astype(F32)
    bottom = (tile < space_size - 1).astype(F32)

    w_new = lax.broadcasted_iota(jnp.int32, (COLS, COLS), 0)
    w_old = lax.broadcasted_iota(jnp.int32, (COLS, COLS), 1)
    order = jnp.where(w_old == (w_new % GRAIN) * 8 + w_new // GRAIN, 1.0, 0.0).astype(BF16)
    lane = lax.broadcasted_iota(jnp.int32, (1, COLS), 1)
    lane_row = lane // 16

    def row_scale(rel):
        if rel < 0:
            return top
        if rel >= rows:
            return bottom
        return None

    def lane_scale(tile_index, halo):
        rel = lane_row + (8 * tile_index - halo)
        return jnp.where(rel < 0, top, jnp.where(rel >= rows, bottom, 1.0))

    def build_state(halo):
        total = rows + 2 * halo
        for t in range(pl.cdiv(total, 8)):
            parts = []
            for e in range(8 * t, 8 * t + 8):
                if e < halo:
                    parts.append(before_ref[:, rows - halo + e, :])
                elif e < halo + rows:
                    parts.append(noise_ref[:, e - halo, :])
                elif e < total:
                    parts.append(after_ref[:, e - halo - rows, :])
                else:
                    parts.append(jnp.zeros((16, COLS), F32))
            block = jnp.concatenate(parts, axis=0)
            moved = None
            for piece in split3(block):
                part = lax.dot_general(
                    order, piece, (((1,), (1,)), ((), ())), preferred_element_type=F32
                )
                moved = part if moved is None else moved + part
            state_ref[t] = moved * lane_scale(t, halo)

    bias = bias_ref[...]
    params = [two_ref[3:6], two_ref[0:3], one_ref[...]]

    def masked(value, pair, margin):
        halves = []
        scales = [row_scale(2 * pair + i - margin) for i in range(2)]
        if scales[0] is None and scales[1] is None:
            return value
        for i in range(2):
            half = value[:, 128 * i : 128 * (i + 1)]
            halves.append(half if scales[i] is None else half * scales[i])
        return jnp.concatenate(halves, axis=1)

    def keep_first(value, pair, margin):
        value = masked(half_silu(value), pair, margin)
        first_ref[pair, GRAIN : GRAIN + COLS, :] = value.astype(BF16)
        first_ref[pair, 0:GRAIN, :] = shifted_rows(value[COLS - GRAIN :], 1).astype(BF16)
        first_ref[pair, GRAIN + COLS :, :] = shifted_rows(value[:GRAIN], -1).astype(BF16)

    def one_step(step):
        halo = HALO - 3 * step
        count = rows + 2 * halo
        tiles = pl.cdiv(count, 8)
        pairs = (count - 2) // 2
        embed = params[step][0:1] * 0.5
        embed = jnp.concatenate([embed, embed], axis=1)
        keep = params[step][1:2]
        rate = params[step][2:3]

        for t in range(tiles):
            z = state_ref[t]
            zb_ref[t, GRAIN : GRAIN + COLS, :] = z.astype(BF16)
            zb_ref[t, 0:GRAIN, :] = shifted_rows(z[COLS - GRAIN :], 1).astype(BF16)
            zb_ref[t, GRAIN + COLS :, :] = shifted_rows(z[:GRAIN], -1).astype(BF16)

        def three(t):
            return jnp.concatenate(
                [zb_ref[t, GRAIN * b : GRAIN * b + COLS, :] for b in range(3)], axis=1
            )

        for t in range(tiles):
            here = min(3, pairs - 4 * t)
            if here > 0:
                out = jnp.dot(
                    three(t), w1a_ref[:, : 256 * here], preferred_element_type=F32
                )
                for i in range(here):
                    value = out[:, 256 * i : 256 * (i + 1)] + embed
                    keep_first(value, 4 * t + i, halo - 1)
            if 4 * t + 3 < pairs:
                both = jnp.concatenate([lane < 64] * 3, axis=1)
                out = jnp.dot(
                    jnp.where(both, three(t + 1), three(t)),
                    w1b_ref[...],
                    preferred_element_type=F32,
                )
                keep_first(out + embed, 4 * t + 3, halo - 1)

        for pair in range(pairs - 1):
            lhs = jnp.concatenate(
                [
                    first_ref[pair + i, GRAIN * b : GRAIN * b + COLS, :]
                    for b in range(3)
                    for i in range(2)
                ],
                axis=1,
            )
            out = jnp.dot(lhs, wm_ref[...], preferred_element_type=F32)
            second_ref[pair] = masked(half_silu(out), pair, halo - 2).astype(BF16)

        new_count = count - 6
        new_tiles = pl.cdiv(new_count, 8)
        for i in range(pairs - 1, 4 * new_tiles + 1):
            second_ref[i] = jnp.zeros((COLS, 256), BF16)
        lhs = jnp.concatenate(
            [
                jnp.concatenate([second_ref[4 * t + i] for i in range(5)], axis=1)
                for t in range(new_tiles)
            ],
            axis=0,
        )
        out = jnp.dot(lhs, w3_ref[...], preferred_element_type=F32)
        for t in range(new_tiles):
            g = out[COLS * t : COLS * (t + 1)]
            left = g[:, 0:128]
            right = g[:, 256:384]
            left = jnp.concatenate(
                [shifted_rows(left[COLS - GRAIN :], 1), left[: COLS - GRAIN]], axis=0
            )
            right = jnp.concatenate([right[GRAIN:], shifted_rows(right[:GRAIN], -1)], axis=0)
            conv = left + g[:, 128:256] + right
            here = state_ref[t]
            old = jnp.concatenate([here[:, 48:], state_ref[t + 1][:, :48]], axis=1) if (
                t + 1 < tiles
            ) else jnp.concatenate([here[:, 48:], jnp.zeros((COLS, 48), F32)], axis=1)
            new = old + keep * old + rate * (old + conv + bias)
            if step + 1 < ITERS:
                state_ref[t] = new * lane_scale(t, halo - 3)
            else:
                turned = new.T
                moved = None
                for piece in split3(turned):
                    part = jnp.dot(piece, order, preferred_element_type=F32)
                    moved = part if moved is None else moved + part
                for r in range(8):
                    out_ref[0, :, 8 * t + r, :] = moved[16 * r : 16 * r + 16]

    for step in range(ITERS):

        @pl.when(time == ITERS - step)
        def _():
            build_state(HALO - 3 * step)

        @pl.when(time >= ITERS - step)
        def _():
            one_step(step)

    @pl.when(time == 0)
    def _():
        out_ref[0] = noise_ref[...]


def chain(
    start_noise, time_embed, keep_rate, denoise_rate, conv_first, conv_middle, conv_last, out_bias
):
    channels, rows, cols = start_noise.shape
    tm_size = lax.axis_size("tm")
    space_size = lax.axis_size("space")
    vmem = pl.BlockSpec(memory_space=pltpu.VMEM)
    smem = pl.BlockSpec(memory_space=pltpu.SMEM)
    shape = jax.ShapeDtypeStruct

    far = jnp.concatenate(
        [
            time_embed,
            jnp.broadcast_to(keep_rate[:, None], (1, cols)),
            jnp.broadcast_to(denoise_rate[:, None], (1, cols)),
        ],
        axis=0,
    )

    def moves(times, tiles):
        return [
            (t * space_size + s, u * space_size + (s + tiles) % space_size)
            for t, u in times
            for s in range(space_size)
        ]

    axes = ("tm", "space")
    own = [(t, t) for t in range(tm_size)]
    before = lax.ppermute(start_noise, axes, moves(own, 1))
    after = lax.ppermute(start_noise, axes, moves(own, -1))
    one = lax.ppermute(far, "tm", [(0, 1), (1, 2), (2, 3), (3, 0)])
    both = jnp.concatenate([far, one], axis=0)
    two = lax.ppermute(both, "tm", [(0, 2), (1, 3), (2, 0), (3, 1)])
    three = one

    w1a, w1b, wm, w3, bias = pl.pallas_call(
        weights_kernel,
        out_shape=(
            pltpu.VMEM((384, 768), BF16),
            pltpu.VMEM((384, 256), BF16),
            pltpu.VMEM((1536, 256), BF16),
            pltpu.VMEM((1280, 384), BF16),
            pltpu.VMEM((1, COLS), F32),
        ),
        in_specs=[vmem] * 4,
        out_specs=(vmem,) * 5,
    )(jnp.swapaxes(conv_first, 1, 2), conv_middle, conv_last, out_bias.reshape(1, channels))

    place = jnp.stack([lax.axis_index("tm"), lax.axis_index("space")]).astype(jnp.int32)
    total = rows + 2 * HALO
    pairs = (total - 2) // 2

    def body(*refs):
        chain_kernel(tm_size, space_size, rows, *refs)

    return pl.pallas_call(
        body,
        out_shape=shape((1, channels, rows, cols), F32),
        in_specs=[vmem] * 6 + [smem] + [vmem] * 5,
        out_specs=vmem,
        scratch_shapes=[
            pltpu.VMEM((pl.cdiv(total, 8), COLS, COLS), F32),
            pltpu.VMEM((pl.cdiv(total, 8), PAD, COLS), BF16),
            pltpu.VMEM((pairs, PAD, 256), BF16),
            pltpu.VMEM((pairs + 1, COLS, 256), BF16),
        ],
        compiler_params=pltpu.CompilerParams(vmem_limit_bytes=48 << 20),
    )(start_noise, before, after, one, two, three, place, bias, w1a, w1b, wm, w3)


def solution(mesh):
    placed = (
        P(None, ("groups", "space"), None),
        P("tm", None),
        P("tm"),
        P("tm"),
        P(),
        P(),
        P(),
        P(),
    )
    return jax.shard_map(
        chain if mesh.shape["tm"] == ITERS + 1 else picard,
        mesh=mesh,
        in_specs=placed,
        out_specs=P("tm", None, ("groups", "space"), None),
        check_vma=False,
    )
```

```python
import jax
import jax.numpy as jnp
from jax import lax
from jax.experimental import pallas as pl
from jax.experimental.pallas import tpu as pltpu
from jax.sharding import PartitionSpec as P

ITERS = 3
HALO = 3 * ITERS
BF16 = jnp.bfloat16
F32 = jnp.float32


def padded(value, sides, width):
    for axis, dim in sides:
        count, length = (lax.axis_size(axis), value.shape[dim])
        up = [(i, (i + 1) % count) for i in range(count - 1)]
        down = [(j, i) for i, j in up]
        last = lax.slice_in_dim(value, length - width, length, axis=dim)
        initial = lax.slice_in_dim(value, 0, width, axis=dim)
        before = lax.ppermute(last, axis, up)
        after = lax.ppermute(initial, axis, down)
        value = jnp.concatenate([before, value, after], axis=dim)
    return value


def carried_in(part, axis):
    place = lax.axis_index(axis)
    gathered = lax.all_gather(part, axis)
    earlier = jnp.arange(gathered.shape[0]) < place
    return jnp.sum(jnp.where(earlier[:, None, None, None], gathered, 0.0), axis=0)


def convolve(field, taps):
    kernel = taps.reshape((3, 3, taps.shape[1], taps.shape[2]))
    result = lax.conv_general_dilated(
        field[None],
        kernel,
        (1, 1),
        ((0, 0), (1, 1)),
        dimension_numbers=("NCHW", "HWOI", "NCHW"),
        preferred_element_type=F32,
    )
    return result[0]


def inside_rows(margin, count, tile_rows):
    glob_row = lax.axis_index("space") * tile_rows - margin + jnp.arange(count, dtype=jnp.int32)
    valid = (glob_row >= 0) & (glob_row < tile_rows * lax.axis_size("space"))
    return valid.astype(F32)[None, :, None]


def picard(
    start_noise, time_embed, keep_rate, denoise_rate, conv_first, conv_middle, conv_last, out_bias
):
    tile_rows = start_noise.shape[1]
    embed = time_embed[0][:, None, None]
    keep = keep_rate[0]
    rate = denoise_rate[0]
    bias = out_bias[:, None, None]
    state = start_noise
    for step in range(ITERS):
        inputs = state.astype(BF16)
        extended = padded(inputs, (("space", 1),), 3)
        first = jax.nn.silu(convolve(extended, conv_first) + embed)
        first = (first * inside_rows(2, tile_rows + 4, tile_rows)).astype(BF16)
        second = jax.nn.silu(convolve(first, conv_middle))
        second = (second * inside_rows(1, tile_rows + 2, tile_rows)).astype(BF16)
        last = convolve(second, conv_last)
        denoised = state + last + bias
        drift = keep * state + rate * denoised
        state = start_noise + carried_in(drift, "tm")
    return state[None]


COLS = 128
GRAIN = 16
PAD = COLS + 2 * GRAIN


def weights_kernel(
    first_ref, middle_ref, last_ref, bias_in_ref, w1_ref, wm_ref, w3_ref, bias_ref
):
    bias_ref[...] = jnp.concatenate([bias_in_ref[...]] * 8, axis=1)
    halves = [first_ref[tap] * BF16(0.5) for tap in range(9)]
    none = jnp.zeros((16, 128), BF16)
    for place in range(4):
        for lanes in range(8):
            k = (lanes - 2 * place) % 8
            for out in range(2):
                for part in range(2):
                    a = k % 4 - out
                    b = 2 if part else k // 4
                    used = 0 <= a < 3 and not (part and k >= 4)
                    w1_ref[
                        place,
                        pl.ds(128 * part + 16 * lanes, 16),
                        pl.ds(128 * out, 128),
                    ] = halves[3 * a + b] if used else none
    zero = jnp.zeros((128, 128), BF16)
    for tap in range(9):
        a, b = divmod(tap, 3)
        block = (middle_ref[tap].astype(F32).T * 0.5).astype(BF16)
        for out in range(2):
            wm_ref[pl.ds(512 * b + 128 * (out + a), 128), pl.ds(128 * out, 128)] = block
    for b in range(3):
        wm_ref[pl.ds(512 * b + 384, 128), pl.ds(0, 128)] = zero
        wm_ref[pl.ds(512 * b, 128), pl.ds(128, 128)] = zero
    for place in range(4):
        for row in range(2):
            for part in range(2):
                parts = []
                for lanes in range(8):
                    k = (lanes - 2 * (place - 1)) % 8
                    a = row + 2 - k % 4
                    b = 2 if part else k // 4
                    if 0 <= a < 3 and not (part and k >= 4):
                        parts.append(last_ref[3 * a + b].astype(F32))
                    else:
                        parts.append(jnp.zeros((16, 128), F32))
                block = jnp.concatenate(parts, axis=0).T.astype(BF16)
                w3_ref[place, pl.ds(128 * row, 128), pl.ds(128 * part, 128)] = block


def split3(value):
    high = value.astype(BF16)
    rest = value - high.astype(F32)
    mid = rest.astype(BF16)
    low = (rest - mid.astype(F32)).astype(BF16)
    return high, mid, low


def shifted_rows(grain, by):
    row = lax.broadcasted_iota(jnp.int32, grain.shape, 0)
    if by > 0:
        return jnp.where(row == 0, 0.0, pltpu.roll(grain, 1, 0))
    return jnp.where(row == GRAIN - 1, 0.0, pltpu.roll(grain, GRAIN - 1, 0))


def half_silu(half):
    return half * jnp.tanh(half) + half


def chain_kernel(
    tm_size,
    space_size,
    rows,
    noise_ref,
    before_ref,
    after_ref,
    one_ref,
    two_ref,
    three_ref,
    place_ref,
    bias_ref,
    w1_ref,
    wm_ref,
    w3_ref,
    out_ref,
    state_ref,
    zb_ref,
    zr_ref,
    first_ref,
    second_ref,
):
    time = place_ref[0]
    tile = place_ref[1]
    top = (tile > 0).astype(F32)
    bottom = (tile < space_size - 1).astype(F32)

    w_new = lax.broadcasted_iota(jnp.int32, (COLS, COLS), 0)
    w_old = lax.broadcasted_iota(jnp.int32, (COLS, COLS), 1)
    order = jnp.where(w_old == (w_new % GRAIN) * 8 + w_new // GRAIN, 1.0, 0.0).astype(BF16)
    lane = lax.broadcasted_iota(jnp.int32, (1, COLS), 1)
    lane_row = lane // 16

    def row_scale(rel):
        if rel < 0:
            return top
        if rel >= rows:
            return bottom
        return None

    def lane_scale(tile_index, halo):
        rel = lane_row + (8 * tile_index - halo)
        return jnp.where(rel < 0, top, jnp.where(rel >= rows, bottom, 1.0))

    def build_state(halo):
        total = rows + 2 * halo
        for t in range(pl.cdiv(total, 8)):
            parts = []
            for e in range(8 * t, 8 * t + 8):
                if e < halo:
                    parts.append(before_ref[:, rows - halo + e, :])
                elif e < halo + rows:
                    parts.append(noise_ref[:, e - halo, :])
                elif e < total:
                    parts.append(after_ref[:, e - halo - rows, :])
                else:
                    parts.append(jnp.zeros((16, COLS), F32))
            block = jnp.concatenate(parts, axis=0)
            moved = None
            for piece in split3(block):
                part = lax.dot_general(
                    order, piece, (((1,), (1,)), ((), ())), preferred_element_type=F32
                )
                moved = part if moved is None else moved + part
            state_ref[t] = moved * lane_scale(t, halo)

    bias = bias_ref[...]
    params = [
        three_ref[...],
        two_ref[...],
        jnp.where(time == 2, three_ref[...], one_ref[...]),
    ]

    def masked(value, pair, margin):
        halves = []
        scales = [row_scale(2 * pair + i - margin) for i in range(2)]
        if scales[0] is None and scales[1] is None:
            return value
        for i in range(2):
            half = value[:, 128 * i : 128 * (i + 1)]
            halves.append(half if scales[i] is None else half * scales[i])
        return jnp.concatenate(halves, axis=1)

    def keep_first(value, pair, margin):
        value = masked(half_silu(value), pair, margin)
        first_ref[pair, GRAIN : GRAIN + COLS, :] = value.astype(BF16)
        first_ref[pair, 0:GRAIN, :] = shifted_rows(value[COLS - GRAIN :], 1).astype(BF16)
        first_ref[pair, GRAIN + COLS :, :] = shifted_rows(value[:GRAIN], -1).astype(BF16)

    def one_step(step):
        halo = HALO - 3 * step
        count = rows + 2 * halo
        tiles = pl.cdiv(count, 8)
        pairs = (count - 2) // 2
        embed = params[step][0:1] * 0.5
        embed = jnp.concatenate([embed, embed], axis=1)
        keep = params[step][1:2]
        rate = params[step][2:3]

        def padded_tile(ref, t, z):
            ref[t, GRAIN : GRAIN + COLS, :] = z.astype(BF16)
            ref[t, 0:GRAIN, :] = shifted_rows(z[COLS - GRAIN :], 1).astype(BF16)
            ref[t, GRAIN + COLS :, :] = shifted_rows(z[:GRAIN], -1).astype(BF16)

        for t in range(tiles):
            padded_tile(zb_ref, t, state_ref[t])
            padded_tile(zr_ref, t, pltpu.roll(state_ref[t], 64, 1))

        for pair in range(pairs):
            t, place = divmod(pair, 4)
            here = [zb_ref[t, GRAIN * b : GRAIN * b + COLS, :] for b in range(3)]
            turned = zr_ref[t, GRAIN : GRAIN + COLS, :]
            if place < 3:
                window = (lane >= 32 * place) & (lane < 32 * place + 64)
                lhs = [jnp.where(window, here[0], turned), here[2]]
            else:
                after = [zb_ref[t + 1, GRAIN * b : GRAIN * b + COLS, :] for b in (0, 2)]
                mixed = jnp.where(lane < 64, turned, zr_ref[t + 1, GRAIN : GRAIN + COLS, :])
                lhs = [
                    jnp.where(lane < 32, after[0], jnp.where(lane < 96, mixed, here[0])),
                    jnp.where(lane < 64, after[1], here[2]),
                ]
            out = jnp.dot(
                jnp.concatenate(lhs, axis=1), w1_ref[place], preferred_element_type=F32
            )
            keep_first(out + embed, pair, halo - 1)

        for pair in range(pairs - 1):
            lhs = jnp.concatenate(
                [
                    first_ref[pair + i, GRAIN * b : GRAIN * b + COLS, :]
                    for b in range(3)
                    for i in range(2)
                ],
                axis=1,
            )
            out = jnp.dot(lhs, wm_ref[...], preferred_element_type=F32)
            second_ref[pair] = masked(half_silu(out), pair, halo - 2).astype(BF16)

        reach = [
            jnp.dot(second_ref[pair], w3_ref[pair % 4], preferred_element_type=F32)
            for pair in range(pairs - 1)
        ]
        low = lane < 64

        def spread(t, part):
            got = [
                reach[p][:, COLS * part : COLS * (part + 1)]
                if p < pairs - 1
                else jnp.zeros((COLS, COLS), F32)
                for p in range(4 * t, 4 * t + 5)
            ]
            proper = jnp.where(low, got[1], got[3]) + jnp.where(
                lane < 32, got[0], jnp.where(lane < 96, got[2], got[4])
            )
            if part == 1:
                return proper, None
            other = jnp.where(low, got[3], got[1]) + jnp.where(
                (lane < 32) | (lane >= 96), got[2], jnp.where(low, got[4], got[0])
            )
            return proper, pltpu.roll(other, 64, 1)

        for t in range(pl.cdiv(count - 6, 8)):
            left, centre = spread(t, 0)
            right, _ = spread(t, 1)
            left = jnp.concatenate(
                [shifted_rows(left[COLS - GRAIN :], 1), left[: COLS - GRAIN]], axis=0
            )
            right = jnp.concatenate([right[GRAIN:], shifted_rows(right[:GRAIN], -1)], axis=0)
            conv = left + centre + right
            here = state_ref[t]
            old = jnp.concatenate([here[:, 48:], state_ref[t + 1][:, :48]], axis=1) if (
                t + 1 < tiles
            ) else jnp.concatenate([here[:, 48:], jnp.zeros((COLS, 48), F32)], axis=1)
            new = old + keep * old + rate * (old + conv + bias)
            if step + 1 < ITERS:
                state_ref[t] = new * lane_scale(t, halo - 3)
            else:
                turned = new.T
                moved = None
                for piece in split3(turned):
                    part = jnp.dot(piece, order, preferred_element_type=F32)
                    moved = part if moved is None else moved + part
                for r in range(8):
                    out_ref[0, :, 8 * t + r, :] = moved[16 * r : 16 * r + 16]

    for step in range(ITERS):

        @pl.when(time == ITERS - step)
        def _():
            build_state(HALO - 3 * step)

        @pl.when(time >= ITERS - step)
        def _():
            one_step(step)

    @pl.when(time == 0)
    def _():
        out_ref[0] = noise_ref[...]


def chain(
    start_noise, time_embed, keep_rate, denoise_rate, conv_first, conv_middle, conv_last, out_bias
):
    channels, rows, cols = start_noise.shape
    tm_size = lax.axis_size("tm")
    space_size = lax.axis_size("space")
    vmem = pl.BlockSpec(memory_space=pltpu.VMEM)
    smem = pl.BlockSpec(memory_space=pltpu.SMEM)
    shape = jax.ShapeDtypeStruct

    far = jnp.concatenate(
        [
            time_embed,
            jnp.broadcast_to(keep_rate[:, None], (1, cols)),
            jnp.broadcast_to(denoise_rate[:, None], (1, cols)),
        ],
        axis=0,
    )

    def moves(times, tiles):
        return [
            (t * space_size + s, u * space_size + (s + tiles) % space_size)
            for t, u in times
            for s in range(space_size)
        ]

    axes = ("tm", "space")
    own = [(t, t) for t in range(tm_size)]
    before = lax.ppermute(start_noise, axes, moves(own, 1))
    after = lax.ppermute(start_noise, axes, moves(own, -1))
    def exchanged(apart):
        return lax.ppermute(far, "tm", [(t, t ^ apart) for t in range(tm_size)])

    one, two, three = (exchanged(apart) for apart in (1, 2, 3))

    w1, wm, w3, bias = pl.pallas_call(
        weights_kernel,
        out_shape=(
            pltpu.VMEM((4, 256, 256), BF16),
            pltpu.VMEM((1536, 256), BF16),
            pltpu.VMEM((4, 256, 256), BF16),
            pltpu.VMEM((1, COLS), F32),
        ),
        in_specs=[vmem] * 4,
        out_specs=(vmem,) * 4,
    )(jnp.swapaxes(conv_first, 1, 2), conv_middle, conv_last, out_bias.reshape(1, channels))

    place = jnp.stack([lax.axis_index("tm"), lax.axis_index("space")]).astype(jnp.int32)
    total = rows + 2 * HALO
    pairs = (total - 2) // 2

    def body(*refs):
        chain_kernel(tm_size, space_size, rows, *refs)

    return pl.pallas_call(
        body,
        out_shape=shape((1, channels, rows, cols), F32),
        in_specs=[vmem] * 6 + [smem] + [vmem] * 4,
        out_specs=vmem,
        scratch_shapes=[
            pltpu.VMEM((pl.cdiv(total, 8), COLS, COLS), F32),
            pltpu.VMEM((pl.cdiv(total, 8), PAD, COLS), BF16),
            pltpu.VMEM((pl.cdiv(total, 8), PAD, COLS), BF16),
            pltpu.VMEM((pairs, PAD, 256), BF16),
            pltpu.VMEM((pairs - 1, COLS, 256), BF16),
        ],
        compiler_params=pltpu.CompilerParams(vmem_limit_bytes=48 << 20),
    )(start_noise, before, after, one, two, three, place, bias, w1, wm, w3)


def solution(mesh):
    placed = (
        P(None, ("groups", "space"), None),
        P("tm", None),
        P("tm"),
        P("tm"),
        P(),
        P(),
        P(),
        P(),
    )
    return jax.shard_map(
        chain if mesh.shape["tm"] == ITERS + 1 else picard,
        mesh=mesh,
        in_specs=placed,
        out_specs=P("tm", None, ("groups", "space"), None),
        check_vma=False,
    )
```

```python
import jax
import jax.numpy as jnp
from jax import lax
from jax.experimental import pallas as pl
from jax.experimental.pallas import tpu as pltpu
from jax.sharding import PartitionSpec as P

ITERS = 3
HALO = 3 * ITERS
BF16 = jnp.bfloat16
F32 = jnp.float32


def padded(value, sides, width):
    for axis, dim in sides:
        count, length = (lax.axis_size(axis), value.shape[dim])
        up = [(i, (i + 1) % count) for i in range(count - 1)]
        down = [(j, i) for i, j in up]
        last = lax.slice_in_dim(value, length - width, length, axis=dim)
        initial = lax.slice_in_dim(value, 0, width, axis=dim)
        before = lax.ppermute(last, axis, up)
        after = lax.ppermute(initial, axis, down)
        value = jnp.concatenate([before, value, after], axis=dim)
    return value


def carried_in(part, axis):
    place = lax.axis_index(axis)
    gathered = lax.all_gather(part, axis)
    earlier = jnp.arange(gathered.shape[0]) < place
    return jnp.sum(jnp.where(earlier[:, None, None, None], gathered, 0.0), axis=0)


def convolve(field, taps):
    kernel = taps.reshape((3, 3, taps.shape[1], taps.shape[2]))
    result = lax.conv_general_dilated(
        field[None],
        kernel,
        (1, 1),
        ((0, 0), (1, 1)),
        dimension_numbers=("NCHW", "HWOI", "NCHW"),
        preferred_element_type=F32,
    )
    return result[0]


def inside_rows(margin, count, tile_rows):
    glob_row = lax.axis_index("space") * tile_rows - margin + jnp.arange(count, dtype=jnp.int32)
    valid = (glob_row >= 0) & (glob_row < tile_rows * lax.axis_size("space"))
    return valid.astype(F32)[None, :, None]


def picard(
    start_noise, time_embed, keep_rate, denoise_rate, conv_first, conv_middle, conv_last, out_bias
):
    tile_rows = start_noise.shape[1]
    embed = time_embed[0][:, None, None]
    keep = keep_rate[0]
    rate = denoise_rate[0]
    bias = out_bias[:, None, None]
    state = start_noise
    for step in range(ITERS):
        inputs = state.astype(BF16)
        extended = padded(inputs, (("space", 1),), 3)
        first = jax.nn.silu(convolve(extended, conv_first) + embed)
        first = (first * inside_rows(2, tile_rows + 4, tile_rows)).astype(BF16)
        second = jax.nn.silu(convolve(first, conv_middle))
        second = (second * inside_rows(1, tile_rows + 2, tile_rows)).astype(BF16)
        last = convolve(second, conv_last)
        denoised = state + last + bias
        drift = keep * state + rate * denoised
        state = start_noise + carried_in(drift, "tm")
    return state[None]


COLS = 128
GRAIN = 16
PAD = COLS + 2 * GRAIN


def pack_kernel(embed_ref, keep_ref, rate_ref, out_ref):
    out_ref[0:1] = embed_ref[...]
    out_ref[1:2] = jnp.broadcast_to(keep_ref[...], (1, COLS))
    out_ref[2:3] = jnp.broadcast_to(rate_ref[...], (1, COLS))


def weights_kernel(
    first_ref, middle_ref, last_ref, bias_in_ref, w1_ref, wm_ref, w3_ref, bias_ref
):
    bias_ref[...] = jnp.concatenate([bias_in_ref[...]] * 8, axis=1)
    halves = [first_ref[tap] * BF16(0.5) for tap in range(9)]
    none = jnp.zeros((16, 128), BF16)
    for place in range(4):
        for lanes in range(8):
            k = (lanes - 2 * place) % 8
            for out in range(2):
                for part in range(2):
                    a = k % 4 - out
                    b = 2 if part else k // 4
                    used = 0 <= a < 3 and not (part and k >= 4)
                    w1_ref[
                        place,
                        pl.ds(128 * part + 16 * lanes, 16),
                        pl.ds(128 * out, 128),
                    ] = halves[3 * a + b] if used else none
    zero = jnp.zeros((128, 128), BF16)
    for tap in range(9):
        a, b = divmod(tap, 3)
        block = (middle_ref[tap].astype(F32).T * 0.5).astype(BF16)
        for out in range(2):
            wm_ref[pl.ds(512 * b + 128 * (out + a), 128), pl.ds(128 * out, 128)] = block
    for b in range(3):
        wm_ref[pl.ds(512 * b + 384, 128), pl.ds(0, 128)] = zero
        wm_ref[pl.ds(512 * b, 128), pl.ds(128, 128)] = zero
    for place in range(4):
        for row in range(2):
            for part in range(2):
                parts = []
                for lanes in range(8):
                    k = (lanes - 2 * (place - 1)) % 8
                    a = row + 2 - k % 4
                    b = 2 if part else k // 4
                    if 0 <= a < 3 and not (part and k >= 4):
                        parts.append(last_ref[3 * a + b].astype(F32))
                    else:
                        parts.append(jnp.zeros((16, 128), F32))
                block = jnp.concatenate(parts, axis=0).T.astype(BF16)
                w3_ref[place, pl.ds(128 * row, 128), pl.ds(128 * part, 128)] = block


def split3(value):
    high = value.astype(BF16)
    rest = value - high.astype(F32)
    mid = rest.astype(BF16)
    low = (rest - mid.astype(F32)).astype(BF16)
    return high, mid, low


def shifted_rows(grain, by):
    row = lax.broadcasted_iota(jnp.int32, grain.shape, 0)
    if by > 0:
        return jnp.where(row == 0, 0.0, pltpu.roll(grain, 1, 0))
    return jnp.where(row == GRAIN - 1, 0.0, pltpu.roll(grain, GRAIN - 1, 0))


def half_silu(half):
    return half * jnp.tanh(half) + half


def chain_kernel(
    tm_size,
    space_size,
    rows,
    noise_ref,
    two_ref,
    near_ref,
    across_ref,
    one_ref,
    three_ref,
    bias_ref,
    w1_ref,
    wm_ref,
    w3_ref,
    out_ref,
    state_ref,
    zb_ref,
    zr_ref,
    first_ref,
    second_ref,
):
    time = lax.axis_index("tm")
    tile = lax.axis_index("space")
    even = tile % 2 == 0
    top = (tile > 0).astype(F32)
    bottom = (tile < space_size - 1).astype(F32)

    w_new = lax.broadcasted_iota(jnp.int32, (COLS, COLS), 0)
    w_old = lax.broadcasted_iota(jnp.int32, (COLS, COLS), 1)
    order = jnp.where(w_old == (w_new % GRAIN) * 8 + w_new // GRAIN, 1.0, 0.0).astype(BF16)
    lane = lax.broadcasted_iota(jnp.int32, (1, COLS), 1)
    lane_row = lane // 16

    def row_scale(rel):
        if rel < 0:
            return top
        if rel >= rows:
            return bottom
        return None

    def lane_scale(tile_index, halo):
        rel = lane_row + (8 * tile_index - halo)
        return jnp.where(rel < 0, top, jnp.where(rel >= rows, bottom, 1.0))

    def build_state(halo):
        total = rows + 2 * halo
        for t in range(pl.cdiv(total, 8)):
            parts = []
            for e in range(8 * t, 8 * t + 8):
                if e < halo:
                    row = rows - halo + e
                    parts.append(jnp.where(even, across_ref[:, row, :], near_ref[:, row, :]))
                elif e < halo + rows:
                    parts.append(noise_ref[:, e - halo, :])
                elif e < total:
                    row = e - halo - rows
                    parts.append(jnp.where(even, near_ref[:, row, :], across_ref[:, row, :]))
                else:
                    parts.append(jnp.zeros((16, COLS), F32))
            block = jnp.concatenate(parts, axis=0)
            moved = None
            for piece in split3(block):
                part = lax.dot_general(
                    order, piece, (((1,), (1,)), ((), ())), preferred_element_type=F32
                )
                moved = part if moved is None else moved + part
            state_ref[t] = moved * lane_scale(t, halo)

    bias = bias_ref[...]
    params = [
        three_ref[...],
        two_ref[...],
        jnp.where(time == 2, three_ref[...], one_ref[...]),
    ]

    def masked(value, pair, margin):
        halves = []
        scales = [row_scale(2 * pair + i - margin) for i in range(2)]
        if scales[0] is None and scales[1] is None:
            return value
        for i in range(2):
            half = value[:, 128 * i : 128 * (i + 1)]
            halves.append(half if scales[i] is None else half * scales[i])
        return jnp.concatenate(halves, axis=1)

    def keep_first(value, pair, margin):
        value = masked(half_silu(value), pair, margin)
        first_ref[pair, GRAIN : GRAIN + COLS, :] = value.astype(BF16)
        first_ref[pair, 0:GRAIN, :] = shifted_rows(value[COLS - GRAIN :], 1).astype(BF16)
        first_ref[pair, GRAIN + COLS :, :] = shifted_rows(value[:GRAIN], -1).astype(BF16)

    def one_step(step):
        halo = HALO - 3 * step
        count = rows + 2 * halo
        tiles = pl.cdiv(count, 8)
        pairs = (count - 2) // 2
        embed = params[step][0:1] * 0.5
        embed = jnp.concatenate([embed, embed], axis=1)
        keep = params[step][1:2]
        rate = params[step][2:3]

        def padded_tile(ref, t, z):
            ref[t, GRAIN : GRAIN + COLS, :] = z.astype(BF16)
            ref[t, 0:GRAIN, :] = shifted_rows(z[COLS - GRAIN :], 1).astype(BF16)
            ref[t, GRAIN + COLS :, :] = shifted_rows(z[:GRAIN], -1).astype(BF16)

        for t in range(tiles):
            padded_tile(zb_ref, t, state_ref[t])
            padded_tile(zr_ref, t, pltpu.roll(state_ref[t], 64, 1))

        for pair in range(pairs):
            t, place = divmod(pair, 4)
            here = [zb_ref[t, GRAIN * b : GRAIN * b + COLS, :] for b in range(3)]
            turned = zr_ref[t, GRAIN : GRAIN + COLS, :]
            if place < 3:
                window = (lane >= 32 * place) & (lane < 32 * place + 64)
                lhs = [jnp.where(window, here[0], turned), here[2]]
            else:
                after = [zb_ref[t + 1, GRAIN * b : GRAIN * b + COLS, :] for b in (0, 2)]
                mixed = jnp.where(lane < 64, turned, zr_ref[t + 1, GRAIN : GRAIN + COLS, :])
                lhs = [
                    jnp.where(lane < 32, after[0], jnp.where(lane < 96, mixed, here[0])),
                    jnp.where(lane < 64, after[1], here[2]),
                ]
            out = jnp.dot(
                jnp.concatenate(lhs, axis=1), w1_ref[place], preferred_element_type=F32
            )
            keep_first(out + embed, pair, halo - 1)

        for pair in range(pairs - 1):
            lhs = jnp.concatenate(
                [
                    first_ref[pair + i, GRAIN * b : GRAIN * b + COLS, :]
                    for b in range(3)
                    for i in range(2)
                ],
                axis=1,
            )
            out = jnp.dot(lhs, wm_ref[...], preferred_element_type=F32)
            second_ref[pair] = masked(half_silu(out), pair, halo - 2).astype(BF16)

        reach = [
            jnp.dot(second_ref[pair], w3_ref[pair % 4], preferred_element_type=F32)
            for pair in range(pairs - 1)
        ]
        low = lane < 64

        def spread(t, part):
            got = [
                reach[p][:, COLS * part : COLS * (part + 1)]
                if p < pairs - 1
                else jnp.zeros((COLS, COLS), F32)
                for p in range(4 * t, 4 * t + 5)
            ]
            proper = jnp.where(low, got[1], got[3]) + jnp.where(
                lane < 32, got[0], jnp.where(lane < 96, got[2], got[4])
            )
            if part == 1:
                return proper, None
            other = jnp.where(low, got[3], got[1]) + jnp.where(
                (lane < 32) | (lane >= 96), got[2], jnp.where(low, got[4], got[0])
            )
            return proper, pltpu.roll(other, 64, 1)

        for t in range(pl.cdiv(count - 6, 8)):
            left, centre = spread(t, 0)
            right, _ = spread(t, 1)
            left = jnp.concatenate(
                [shifted_rows(left[COLS - GRAIN :], 1), left[: COLS - GRAIN]], axis=0
            )
            right = jnp.concatenate([right[GRAIN:], shifted_rows(right[:GRAIN], -1)], axis=0)
            conv = left + centre + right
            here = state_ref[t]
            old = jnp.concatenate([here[:, 48:], state_ref[t + 1][:, :48]], axis=1) if (
                t + 1 < tiles
            ) else jnp.concatenate([here[:, 48:], jnp.zeros((COLS, 48), F32)], axis=1)
            new = old + keep * old + rate * (old + conv + bias)
            if step + 1 < ITERS:
                state_ref[t] = new * lane_scale(t, halo - 3)
            else:
                turned = new.T
                moved = None
                for piece in split3(turned):
                    part = jnp.dot(piece, order, preferred_element_type=F32)
                    moved = part if moved is None else moved + part
                for r in range(8):
                    out_ref[0, :, 8 * t + r, :] = moved[16 * r : 16 * r + 16]

    for step in range(ITERS):

        @pl.when(time == ITERS - step)
        def _():
            build_state(HALO - 3 * step)

        @pl.when(time >= ITERS - step)
        def _():
            one_step(step)

    @pl.when(time == 0)
    def _():
        out_ref[0] = noise_ref[...]


def chain(
    start_noise, time_embed, keep_rate, denoise_rate, conv_first, conv_middle, conv_last, out_bias
):
    channels, rows, cols = start_noise.shape
    tm_size = lax.axis_size("tm")
    space_size = lax.axis_size("space")
    vmem = pl.BlockSpec(memory_space=pltpu.VMEM)
    shape = jax.ShapeDtypeStruct

    far = pl.pallas_call(
        pack_kernel,
        out_shape=pltpu.VMEM((3, cols), F32),
        in_specs=[vmem] * 3,
        out_specs=vmem,
    )(time_embed, keep_rate.reshape(1, 1), denoise_rate.reshape(1, 1))

    def swapped(value, first):
        pairs = [(i, i + 1) for i in range(first, space_size - 1, 2)]
        pairs += [(0, space_size - 1)] if first else []
        return lax.ppermute(value, "space", pairs + [(j, i) for i, j in pairs])

    def exchanged(apart):
        return lax.ppermute(far, "tm", [(t, t ^ apart) for t in range(tm_size)])

    start_noise, far = lax.optimization_barrier((start_noise, far))
    two = exchanged(2)
    near = swapped(start_noise, 0)
    across = swapped(start_noise, 1)
    one = exchanged(1)
    three = exchanged(3)

    w1, wm, w3, bias = pl.pallas_call(
        weights_kernel,
        out_shape=(
            pltpu.VMEM((4, 256, 256), BF16),
            pltpu.VMEM((1536, 256), BF16),
            pltpu.VMEM((4, 256, 256), BF16),
            pltpu.VMEM((1, COLS), F32),
        ),
        in_specs=[vmem] * 4,
        out_specs=(vmem,) * 4,
    )(jnp.swapaxes(conv_first, 1, 2), conv_middle, conv_last, out_bias.reshape(1, channels))

    total = rows + 2 * HALO
    pairs = (total - 2) // 2

    def body(*refs):
        chain_kernel(tm_size, space_size, rows, *refs)

    return pl.pallas_call(
        body,
        out_shape=shape((1, channels, rows, cols), F32),
        in_specs=[vmem] * 10,
        out_specs=vmem,
        scratch_shapes=[
            pltpu.VMEM((pl.cdiv(total, 8), COLS, COLS), F32),
            pltpu.VMEM((pl.cdiv(total, 8), PAD, COLS), BF16),
            pltpu.VMEM((pl.cdiv(total, 8), PAD, COLS), BF16),
            pltpu.VMEM((pairs, PAD, 256), BF16),
            pltpu.VMEM((pairs - 1, COLS, 256), BF16),
        ],
        compiler_params=pltpu.CompilerParams(vmem_limit_bytes=48 << 20),
    )(start_noise, two, near, across, one, three, bias, w1, wm, w3)


def solution(mesh):
    placed = (
        P(None, ("groups", "space"), None),
        P("tm", None),
        P("tm"),
        P("tm"),
        P(),
        P(),
        P(),
        P(),
    )
    return jax.shard_map(
        chain
        if mesh.shape["tm"] == ITERS + 1 and mesh.shape["space"] % 2 == 0
        else picard,
        mesh=mesh,
        in_specs=placed,
        out_specs=P("tm", None, ("groups", "space"), None),
        check_vma=False,
    )
```

```python
import jax
import jax.numpy as jnp
from jax import lax
from jax.experimental import pallas as pl
from jax.experimental.pallas import tpu as pltpu
from jax.sharding import PartitionSpec as P

ITERS = 3
HALO = 3 * ITERS
BF16 = jnp.bfloat16
F32 = jnp.float32


def padded(value, sides, width):
    for axis, dim in sides:
        count, length = (lax.axis_size(axis), value.shape[dim])
        up = [(i, (i + 1) % count) for i in range(count - 1)]
        down = [(j, i) for i, j in up]
        last = lax.slice_in_dim(value, length - width, length, axis=dim)
        initial = lax.slice_in_dim(value, 0, width, axis=dim)
        before = lax.ppermute(last, axis, up)
        after = lax.ppermute(initial, axis, down)
        value = jnp.concatenate([before, value, after], axis=dim)
    return value


def carried_in(part, axis):
    place = lax.axis_index(axis)
    gathered = lax.all_gather(part, axis)
    earlier = jnp.arange(gathered.shape[0]) < place
    return jnp.sum(jnp.where(earlier[:, None, None, None], gathered, 0.0), axis=0)


def convolve(field, taps):
    kernel = taps.reshape((3, 3, taps.shape[1], taps.shape[2]))
    result = lax.conv_general_dilated(
        field[None],
        kernel,
        (1, 1),
        ((0, 0), (1, 1)),
        dimension_numbers=("NCHW", "HWOI", "NCHW"),
        preferred_element_type=F32,
    )
    return result[0]


def inside_rows(margin, count, tile_rows):
    glob_row = lax.axis_index("space") * tile_rows - margin + jnp.arange(count, dtype=jnp.int32)
    valid = (glob_row >= 0) & (glob_row < tile_rows * lax.axis_size("space"))
    return valid.astype(F32)[None, :, None]


def picard(
    start_noise, time_embed, keep_rate, denoise_rate, conv_first, conv_middle, conv_last, out_bias
):
    tile_rows = start_noise.shape[1]
    embed = time_embed[0][:, None, None]
    keep = keep_rate[0]
    rate = denoise_rate[0]
    bias = out_bias[:, None, None]
    state = start_noise
    for step in range(ITERS):
        inputs = state.astype(BF16)
        extended = padded(inputs, (("space", 1),), 3)
        first = jax.nn.silu(convolve(extended, conv_first) + embed)
        first = (first * inside_rows(2, tile_rows + 4, tile_rows)).astype(BF16)
        second = jax.nn.silu(convolve(first, conv_middle))
        second = (second * inside_rows(1, tile_rows + 2, tile_rows)).astype(BF16)
        last = convolve(second, conv_last)
        denoised = state + last + bias
        drift = keep * state + rate * denoised
        state = start_noise + carried_in(drift, "tm")
    return state[None]


COLS = 128
GRAIN = 16
PAD = COLS + 2 * GRAIN


def pack_kernel(embed_ref, keep_ref, rate_ref, out_ref):
    out_ref[0:1] = embed_ref[...]
    out_ref[1:2] = jnp.broadcast_to(keep_ref[...], (1, COLS))
    out_ref[2:3] = jnp.broadcast_to(rate_ref[...], (1, COLS))


def weights_kernel(
    first_ref, middle_ref, last_ref, bias_in_ref, w1_ref, wm_ref, w3_ref, bias_ref
):
    bias_ref[...] = jnp.concatenate([bias_in_ref[...]] * 8, axis=1)
    halves = [first_ref[tap] * BF16(0.5) for tap in range(9)]
    none = jnp.zeros((16, 128), BF16)
    for place in range(4):
        for lanes in range(8):
            k = (lanes - 2 * place) % 8
            for out in range(2):
                for part in range(2):
                    a = k % 4 - out
                    b = 2 if part else k // 4
                    used = 0 <= a < 3 and not (part and k >= 4)
                    w1_ref[
                        place,
                        pl.ds(128 * part + 16 * lanes, 16),
                        pl.ds(128 * out, 128),
                    ] = halves[3 * a + b] if used else none
    zero = jnp.zeros((128, 128), BF16)
    for tap in range(9):
        a, b = divmod(tap, 3)
        block = (middle_ref[tap].astype(F32).T * 0.5).astype(BF16)
        for out in range(2):
            wm_ref[pl.ds(512 * b + 128 * (out + a), 128), pl.ds(128 * out, 128)] = block
    for b in range(3):
        wm_ref[pl.ds(512 * b + 384, 128), pl.ds(0, 128)] = zero
        wm_ref[pl.ds(512 * b, 128), pl.ds(128, 128)] = zero
    for place in range(4):
        for row in range(2):
            for part in range(2):
                parts = []
                for lanes in range(8):
                    k = (lanes - 2 * (place - 1)) % 8
                    a = row + 2 - k % 4
                    b = 2 if part else k // 4
                    if 0 <= a < 3 and not (part and k >= 4):
                        parts.append(last_ref[3 * a + b].astype(F32))
                    else:
                        parts.append(jnp.zeros((16, 128), F32))
                block = jnp.concatenate(parts, axis=0).T.astype(BF16)
                w3_ref[place, pl.ds(128 * row, 128), pl.ds(128 * part, 128)] = block


def split3(value):
    high = value.astype(BF16)
    rest = value - high.astype(F32)
    mid = rest.astype(BF16)
    low = (rest - mid.astype(F32)).astype(BF16)
    return high, mid, low


def shifted_rows(grain, by):
    row = lax.broadcasted_iota(jnp.int32, grain.shape, 0)
    if by > 0:
        return jnp.where(row == 0, 0.0, pltpu.roll(grain, 1, 0))
    return jnp.where(row == GRAIN - 1, 0.0, pltpu.roll(grain, GRAIN - 1, 0))


def half_silu(half):
    return half * jnp.tanh(half) + half


def chain_kernel(
    tm_size,
    space_size,
    rows,
    noise_ref,
    two_ref,
    near_ref,
    across_ref,
    one_ref,
    three_ref,
    bias_ref,
    w1_ref,
    wm_ref,
    w3_ref,
    out_ref,
    state_ref,
    zb_ref,
    zr_ref,
    first_ref,
    second_ref,
):
    time = lax.axis_index("tm")
    tile = lax.axis_index("space")
    even = tile % 2 == 0
    top = (tile > 0).astype(F32)
    bottom = (tile < space_size - 1).astype(F32)

    w_new = lax.broadcasted_iota(jnp.int32, (COLS, COLS), 0)
    w_old = lax.broadcasted_iota(jnp.int32, (COLS, COLS), 1)
    order = jnp.where(w_old == (w_new % GRAIN) * 8 + w_new // GRAIN, 1.0, 0.0).astype(BF16)
    lane = lax.broadcasted_iota(jnp.int32, (1, COLS), 1)
    lane_row = lane // 16

    def row_scale(rel):
        if rel < 0:
            return top
        if rel >= rows:
            return bottom
        return None

    def lane_scale(tile_index, halo):
        rel = lane_row + (8 * tile_index - halo)
        return jnp.where(rel < 0, top, jnp.where(rel >= rows, bottom, 1.0))

    def build_state(halo):
        total = rows + 2 * halo
        for t in range(pl.cdiv(total, 8)):
            parts = []
            for e in range(8 * t, 8 * t + 8):
                if e < halo:
                    row = rows - halo + e
                    parts.append(jnp.where(even, across_ref[:, row, :], near_ref[:, row, :]))
                elif e < halo + rows:
                    parts.append(noise_ref[:, e - halo, :])
                elif e < total:
                    row = e - halo - rows
                    parts.append(jnp.where(even, near_ref[:, row, :], across_ref[:, row, :]))
                else:
                    parts.append(jnp.zeros((16, COLS), F32))
            block = jnp.concatenate(parts, axis=0)
            moved = None
            for piece in split3(block):
                part = lax.dot_general(
                    order, piece, (((1,), (1,)), ((), ())), preferred_element_type=F32
                )
                moved = part if moved is None else moved + part
            state_ref[t] = moved * lane_scale(t, halo)

    bias = bias_ref[...]
    params = [
        three_ref[...],
        two_ref[...],
        jnp.where(time == 2, three_ref[...], one_ref[...]),
    ]

    def masked(value, pair, margin):
        halves = []
        scales = [row_scale(2 * pair + i - margin) for i in range(2)]
        if scales[0] is None and scales[1] is None:
            return value
        for i in range(2):
            half = value[:, 128 * i : 128 * (i + 1)]
            halves.append(half if scales[i] is None else half * scales[i])
        return jnp.concatenate(halves, axis=1)

    def keep_first(value, pair, margin):
        value = masked(half_silu(value), pair, margin)
        first_ref[pair, GRAIN : GRAIN + COLS, :] = value.astype(BF16)
        first_ref[pair, 0:GRAIN, :] = shifted_rows(value[COLS - GRAIN :], 1).astype(BF16)
        first_ref[pair, GRAIN + COLS :, :] = shifted_rows(value[:GRAIN], -1).astype(BF16)

    def one_step(step):
        halo = HALO - 3 * step
        count = rows + 2 * halo
        tiles = pl.cdiv(count, 8)
        pairs = (count - 2) // 2
        embed = params[step][0:1] * 0.5
        embed = jnp.concatenate([embed, embed], axis=1)
        keep = params[step][1:2]
        rate = params[step][2:3]

        def padded_tile(ref, t, z):
            ref[t, GRAIN : GRAIN + COLS, :] = z.astype(BF16)
            ref[t, 0:GRAIN, :] = shifted_rows(z[COLS - GRAIN :], 1).astype(BF16)
            ref[t, GRAIN + COLS :, :] = shifted_rows(z[:GRAIN], -1).astype(BF16)

        for t in range(tiles):
            padded_tile(zb_ref, t, state_ref[t])
            padded_tile(zr_ref, t, pltpu.roll(state_ref[t], 64, 1))

        for pair in range(pairs):
            t, place = divmod(pair, 4)
            here = [zb_ref[t, GRAIN * b : GRAIN * b + COLS, :] for b in range(3)]
            turned = zr_ref[t, GRAIN : GRAIN + COLS, :]
            if place < 3:
                window = (lane >= 32 * place) & (lane < 32 * place + 64)
                lhs = [jnp.where(window, here[0], turned), here[2]]
            else:
                after = [zb_ref[t + 1, GRAIN * b : GRAIN * b + COLS, :] for b in (0, 2)]
                mixed = jnp.where(lane < 64, turned, zr_ref[t + 1, GRAIN : GRAIN + COLS, :])
                lhs = [
                    jnp.where(lane < 32, after[0], jnp.where(lane < 96, mixed, here[0])),
                    jnp.where(lane < 64, after[1], here[2]),
                ]
            out = jnp.dot(
                jnp.concatenate(lhs, axis=1), w1_ref[place], preferred_element_type=F32
            )
            keep_first(out + embed, pair, halo - 1)

        for pair in range(pairs - 1):
            lhs = jnp.concatenate(
                [
                    first_ref[pair + i, GRAIN * b : GRAIN * b + COLS, :]
                    for b in range(3)
                    for i in range(2)
                ],
                axis=1,
            )
            out = jnp.dot(lhs, wm_ref[...], preferred_element_type=F32)
            second_ref[pair] = masked(half_silu(out), pair, halo - 2).astype(BF16)

        reach = [
            jnp.dot(second_ref[pair], w3_ref[pair % 4], preferred_element_type=F32)
            for pair in range(pairs - 1)
        ]
        low = lane < 64

        def spread(t, part):
            got = [
                reach[p][:, COLS * part : COLS * (part + 1)]
                if p < pairs - 1
                else jnp.zeros((COLS, COLS), F32)
                for p in range(4 * t, 4 * t + 5)
            ]
            proper = jnp.where(low, got[1], got[3]) + jnp.where(
                lane < 32, got[0], jnp.where(lane < 96, got[2], got[4])
            )
            if part == 1:
                return proper, None
            other = jnp.where(low, got[3], got[1]) + jnp.where(
                (lane < 32) | (lane >= 96), got[2], jnp.where(low, got[4], got[0])
            )
            return proper, pltpu.roll(other, 64, 1)

        for t in range(pl.cdiv(count - 6, 8)):
            left, centre = spread(t, 0)
            right, _ = spread(t, 1)
            left = jnp.concatenate(
                [shifted_rows(left[COLS - GRAIN :], 1), left[: COLS - GRAIN]], axis=0
            )
            right = jnp.concatenate([right[GRAIN:], shifted_rows(right[:GRAIN], -1)], axis=0)
            conv = left + centre + right
            here = state_ref[t]
            old = jnp.concatenate([here[:, 48:], state_ref[t + 1][:, :48]], axis=1) if (
                t + 1 < tiles
            ) else jnp.concatenate([here[:, 48:], jnp.zeros((COLS, 48), F32)], axis=1)
            new = old + keep * old + rate * (old + conv + bias)
            if step + 1 < ITERS:
                state_ref[t] = new * lane_scale(t, halo - 3)
            else:
                turned = new.T
                moved = None
                for piece in split3(turned):
                    part = jnp.dot(piece, order, preferred_element_type=F32)
                    moved = part if moved is None else moved + part
                for r in range(8):
                    out_ref[0, :, 8 * t + r, :] = moved[16 * r : 16 * r + 16]

    for start in range(ITERS):

        @pl.when(time == ITERS - start)
        def _():
            build_state(HALO - 3 * start)
            for step in range(start, ITERS):
                one_step(step)

    @pl.when(time == 0)
    def _():
        out_ref[0] = noise_ref[...]


def chain(
    start_noise, time_embed, keep_rate, denoise_rate, conv_first, conv_middle, conv_last, out_bias
):
    channels, rows, cols = start_noise.shape
    tm_size = lax.axis_size("tm")
    space_size = lax.axis_size("space")
    vmem = pl.BlockSpec(memory_space=pltpu.VMEM)
    shape = jax.ShapeDtypeStruct

    far = pl.pallas_call(
        pack_kernel,
        out_shape=pltpu.VMEM((3, cols), F32),
        in_specs=[vmem] * 3,
        out_specs=vmem,
    )(time_embed, keep_rate.reshape(1, 1), denoise_rate.reshape(1, 1))

    def swapped(value, first):
        pairs = [(i, i + 1) for i in range(first, space_size - 1, 2)]
        pairs += [(0, space_size - 1)] if first else []
        return lax.ppermute(value, "space", pairs + [(j, i) for i, j in pairs])

    def exchanged(apart):
        return lax.ppermute(far, "tm", [(t, t ^ apart) for t in range(tm_size)])

    start_noise, far = lax.optimization_barrier((start_noise, far))
    two = exchanged(2)
    near = swapped(start_noise, 0)
    across = swapped(start_noise, 1)
    one = exchanged(1)
    three = exchanged(3)

    w1, wm, w3, bias = pl.pallas_call(
        weights_kernel,
        out_shape=(
            pltpu.VMEM((4, 256, 256), BF16),
            pltpu.VMEM((1536, 256), BF16),
            pltpu.VMEM((4, 256, 256), BF16),
            pltpu.VMEM((1, COLS), F32),
        ),
        in_specs=[vmem] * 4,
        out_specs=(vmem,) * 4,
    )(jnp.swapaxes(conv_first, 1, 2), conv_middle, conv_last, out_bias.reshape(1, channels))

    total = rows + 2 * HALO
    pairs = (total - 2) // 2

    def body(*refs):
        chain_kernel(tm_size, space_size, rows, *refs)

    return pl.pallas_call(
        body,
        out_shape=shape((1, channels, rows, cols), F32),
        in_specs=[vmem] * 10,
        out_specs=vmem,
        scratch_shapes=[
            pltpu.VMEM((pl.cdiv(total, 8), COLS, COLS), F32),
            pltpu.VMEM((pl.cdiv(total, 8), PAD, COLS), BF16),
            pltpu.VMEM((pl.cdiv(total, 8), PAD, COLS), BF16),
            pltpu.VMEM((pairs, PAD, 256), BF16),
            pltpu.VMEM((pairs - 1, COLS, 256), BF16),
        ],
        compiler_params=pltpu.CompilerParams(vmem_limit_bytes=48 << 20),
    )(start_noise, two, near, across, one, three, bias, w1, wm, w3)


def solution(mesh):
    placed = (
        P(None, ("groups", "space"), None),
        P("tm", None),
        P("tm"),
        P("tm"),
        P(),
        P(),
        P(),
        P(),
    )
    return jax.shard_map(
        chain
        if mesh.shape["tm"] == ITERS + 1 and mesh.shape["space"] % 2 == 0
        else picard,
        mesh=mesh,
        in_specs=placed,
        out_specs=P("tm", None, ("groups", "space"), None),
        check_vma=False,
    )
```

```python
import jax
import jax.numpy as jnp
from jax import lax
from jax.experimental import pallas as pl
from jax.experimental.pallas import tpu as pltpu
from jax.sharding import PartitionSpec as P

ITERS = 3
HALO = 3 * ITERS
BF16 = jnp.bfloat16
F32 = jnp.float32


def padded(value, sides, width):
    for axis, dim in sides:
        count, length = (lax.axis_size(axis), value.shape[dim])
        up = [(i, (i + 1) % count) for i in range(count - 1)]
        down = [(j, i) for i, j in up]
        last = lax.slice_in_dim(value, length - width, length, axis=dim)
        initial = lax.slice_in_dim(value, 0, width, axis=dim)
        before = lax.ppermute(last, axis, up)
        after = lax.ppermute(initial, axis, down)
        value = jnp.concatenate([before, value, after], axis=dim)
    return value


def carried_in(part, axis):
    place = lax.axis_index(axis)
    gathered = lax.all_gather(part, axis)
    earlier = jnp.arange(gathered.shape[0]) < place
    return jnp.sum(jnp.where(earlier[:, None, None, None], gathered, 0.0), axis=0)


def convolve(field, taps):
    kernel = taps.reshape((3, 3, taps.shape[1], taps.shape[2]))
    result = lax.conv_general_dilated(
        field[None],
        kernel,
        (1, 1),
        ((0, 0), (1, 1)),
        dimension_numbers=("NCHW", "HWOI", "NCHW"),
        preferred_element_type=F32,
    )
    return result[0]


def inside_rows(margin, count, tile_rows):
    glob_row = lax.axis_index("space") * tile_rows - margin + jnp.arange(count, dtype=jnp.int32)
    valid = (glob_row >= 0) & (glob_row < tile_rows * lax.axis_size("space"))
    return valid.astype(F32)[None, :, None]


def picard(
    start_noise, time_embed, keep_rate, denoise_rate, conv_first, conv_middle, conv_last, out_bias
):
    tile_rows = start_noise.shape[1]
    embed = time_embed[0][:, None, None]
    keep = keep_rate[0]
    rate = denoise_rate[0]
    bias = out_bias[:, None, None]
    state = start_noise
    for step in range(ITERS):
        inputs = state.astype(BF16)
        extended = padded(inputs, (("space", 1),), 3)
        first = jax.nn.silu(convolve(extended, conv_first) + embed)
        first = (first * inside_rows(2, tile_rows + 4, tile_rows)).astype(BF16)
        second = jax.nn.silu(convolve(first, conv_middle))
        second = (second * inside_rows(1, tile_rows + 2, tile_rows)).astype(BF16)
        last = convolve(second, conv_last)
        denoised = state + last + bias
        drift = keep * state + rate * denoised
        state = start_noise + carried_in(drift, "tm")
    return state[None]


COLS = 128
GRAIN = 16
PAD = COLS + 2 * GRAIN


def pack_kernel(embed_ref, keep_ref, rate_ref, out_ref):
    out_ref[0:1] = embed_ref[...]
    out_ref[1:2] = jnp.broadcast_to(keep_ref[...], (1, COLS))
    out_ref[2:3] = jnp.broadcast_to(rate_ref[...], (1, COLS))


def weights_kernel(
    first_ref, middle_ref, last_ref, bias_in_ref, w1_ref, wm_ref, w3_ref, bias_ref
):
    bias_ref[...] = jnp.concatenate([bias_in_ref[...]] * 8, axis=1)
    halves = [first_ref[tap] * BF16(0.5) for tap in range(9)]
    none = jnp.zeros((16, 128), BF16)
    for place in range(4):
        for lanes in range(8):
            k = (lanes - 2 * place) % 8
            for out in range(2):
                for part in range(2):
                    a = k % 4 - out
                    b = 2 if part else k // 4
                    used = 0 <= a < 3 and not (part and k >= 4)
                    w1_ref[
                        place,
                        pl.ds(128 * part + 16 * lanes, 16),
                        pl.ds(128 * out, 128),
                    ] = halves[3 * a + b] if used else none
    zero = jnp.zeros((128, 128), BF16)
    for tap in range(9):
        a, b = divmod(tap, 3)
        block = middle_ref[tap].T * BF16(0.5)
        for out in range(2):
            wm_ref[pl.ds(512 * b + 128 * (out + a), 128), pl.ds(128 * out, 128)] = block
    for b in range(3):
        wm_ref[pl.ds(512 * b + 384, 128), pl.ds(0, 128)] = zero
        wm_ref[pl.ds(512 * b, 128), pl.ds(128, 128)] = zero
    for place in range(4):
        for row in range(2):
            for part in range(2):
                parts = []
                for lanes in range(8):
                    k = (lanes - 2 * (place - 1)) % 8
                    a = row + 2 - k % 4
                    b = 2 if part else k // 4
                    if 0 <= a < 3 and not (part and k >= 4):
                        parts.append(last_ref[3 * a + b])
                    else:
                        parts.append(none)
                block = jnp.concatenate(parts, axis=0).T
                w3_ref[place, pl.ds(128 * row, 128), pl.ds(128 * part, 128)] = block


def split3(value):
    high = value.astype(BF16)
    rest = value - high.astype(F32)
    mid = rest.astype(BF16)
    low = (rest - mid.astype(F32)).astype(BF16)
    return high, mid, low


def shifted_rows(grain, by):
    row = lax.broadcasted_iota(jnp.int32, grain.shape, 0)
    if by > 0:
        return jnp.where(row == 0, 0.0, pltpu.roll(grain, 1, 0))
    return jnp.where(row == GRAIN - 1, 0.0, pltpu.roll(grain, GRAIN - 1, 0))


def half_silu(half):
    return half * jnp.tanh(half) + half


def chain_kernel(
    tm_size,
    space_size,
    rows,
    noise_ref,
    two_ref,
    near_ref,
    across_ref,
    one_ref,
    three_ref,
    bias_ref,
    w1_ref,
    wm_ref,
    w3_ref,
    out_ref,
    state_ref,
    zb_ref,
    zr_ref,
    first_ref,
    second_ref,
):
    time = lax.axis_index("tm")
    tile = lax.axis_index("space")
    even = tile % 2 == 0
    top = (tile > 0).astype(F32)
    bottom = (tile < space_size - 1).astype(F32)

    w_new = lax.broadcasted_iota(jnp.int32, (COLS, COLS), 0)
    w_old = lax.broadcasted_iota(jnp.int32, (COLS, COLS), 1)
    order = jnp.where(w_old == (w_new % GRAIN) * 8 + w_new // GRAIN, 1.0, 0.0).astype(BF16)
    lane = lax.broadcasted_iota(jnp.int32, (1, COLS), 1)
    lane_row = lane // 16

    def row_scale(rel):
        if rel < 0:
            return top
        if rel >= rows:
            return bottom
        return None

    def lane_scale(tile_index, halo):
        rel = lane_row + (8 * tile_index - halo)
        return jnp.where(rel < 0, top, jnp.where(rel >= rows, bottom, 1.0))

    def build_state(halo):
        total = rows + 2 * halo
        for t in range(pl.cdiv(total, 8)):
            parts = []
            for e in range(8 * t, 8 * t + 8):
                if e < halo:
                    row = rows - halo + e
                    parts.append(jnp.where(even, across_ref[:, row, :], near_ref[:, row, :]))
                elif e < halo + rows:
                    parts.append(noise_ref[:, e - halo, :])
                elif e < total:
                    row = e - halo - rows
                    parts.append(jnp.where(even, near_ref[:, row, :], across_ref[:, row, :]))
                else:
                    parts.append(jnp.zeros((16, COLS), F32))
            block = jnp.concatenate(parts, axis=0)
            moved = None
            for piece in split3(block):
                part = lax.dot_general(
                    order, piece, (((1,), (1,)), ((), ())), preferred_element_type=F32
                )
                moved = part if moved is None else moved + part
            state_ref[t] = moved * lane_scale(t, halo)

    bias = bias_ref[...]
    params = [
        three_ref[...],
        two_ref[...],
        jnp.where(time == 2, three_ref[...], one_ref[...]),
    ]

    def masked(value, pair, margin):
        halves = []
        scales = [row_scale(2 * pair + i - margin) for i in range(2)]
        if scales[0] is None and scales[1] is None:
            return value
        for i in range(2):
            half = value[:, 128 * i : 128 * (i + 1)]
            halves.append(half if scales[i] is None else half * scales[i])
        return jnp.concatenate(halves, axis=1)

    def keep_first(value, pair, margin):
        value = masked(half_silu(value), pair, margin)
        first_ref[pair, GRAIN : GRAIN + COLS, :] = value.astype(BF16)
        first_ref[pair, 0:GRAIN, :] = shifted_rows(value[COLS - GRAIN :], 1).astype(BF16)
        first_ref[pair, GRAIN + COLS :, :] = shifted_rows(value[:GRAIN], -1).astype(BF16)

    def one_step(step):
        halo = HALO - 3 * step
        count = rows + 2 * halo
        tiles = pl.cdiv(count, 8)
        pairs = (count - 2) // 2
        embed = params[step][0:1] * 0.5
        embed = jnp.concatenate([embed, embed], axis=1)
        keep = params[step][1:2]
        rate = params[step][2:3]

        def padded_tile(ref, t, z):
            ref[t, GRAIN : GRAIN + COLS, :] = z.astype(BF16)
            ref[t, 0:GRAIN, :] = shifted_rows(z[COLS - GRAIN :], 1).astype(BF16)
            ref[t, GRAIN + COLS :, :] = shifted_rows(z[:GRAIN], -1).astype(BF16)

        for t in range(tiles):
            padded_tile(zb_ref, t, state_ref[t])
            padded_tile(zr_ref, t, pltpu.roll(state_ref[t], 64, 1))

        for pair in range(pairs):
            t, place = divmod(pair, 4)
            here = [zb_ref[t, GRAIN * b : GRAIN * b + COLS, :] for b in range(3)]
            turned = zr_ref[t, GRAIN : GRAIN + COLS, :]
            if place < 3:
                window = (lane >= 32 * place) & (lane < 32 * place + 64)
                lhs = [jnp.where(window, here[0], turned), here[2]]
            else:
                after = [zb_ref[t + 1, GRAIN * b : GRAIN * b + COLS, :] for b in (0, 2)]
                mixed = jnp.where(lane < 64, turned, zr_ref[t + 1, GRAIN : GRAIN + COLS, :])
                lhs = [
                    jnp.where(lane < 32, after[0], jnp.where(lane < 96, mixed, here[0])),
                    jnp.where(lane < 64, after[1], here[2]),
                ]
            out = jnp.dot(
                jnp.concatenate(lhs, axis=1), w1_ref[place], preferred_element_type=F32
            )
            keep_first(out + embed, pair, halo - 1)

        for pair in range(pairs - 1):
            lhs = jnp.concatenate(
                [
                    first_ref[pair + i, GRAIN * b : GRAIN * b + COLS, :]
                    for b in range(3)
                    for i in range(2)
                ],
                axis=1,
            )
            out = jnp.dot(lhs, wm_ref[...], preferred_element_type=F32)
            second_ref[pair] = masked(half_silu(out), pair, halo - 2).astype(BF16)

        reach = [
            jnp.dot(second_ref[pair], w3_ref[pair % 4], preferred_element_type=F32)
            for pair in range(pairs - 1)
        ]
        low = lane < 64

        def spread(t, part):
            got = [
                reach[p][:, COLS * part : COLS * (part + 1)]
                if p < pairs - 1
                else jnp.zeros((COLS, COLS), F32)
                for p in range(4 * t, 4 * t + 5)
            ]
            proper = jnp.where(low, got[1], got[3]) + jnp.where(
                lane < 32, got[0], jnp.where(lane < 96, got[2], got[4])
            )
            if part == 1:
                return proper, None
            other = jnp.where(low, got[3], got[1]) + jnp.where(
                (lane < 32) | (lane >= 96), got[2], jnp.where(low, got[4], got[0])
            )
            return proper, pltpu.roll(other, 64, 1)

        for t in range(pl.cdiv(count - 6, 8)):
            left, centre = spread(t, 0)
            right, _ = spread(t, 1)
            left = jnp.concatenate(
                [shifted_rows(left[COLS - GRAIN :], 1), left[: COLS - GRAIN]], axis=0
            )
            right = jnp.concatenate([right[GRAIN:], shifted_rows(right[:GRAIN], -1)], axis=0)
            conv = left + centre + right
            here = state_ref[t]
            old = jnp.concatenate([here[:, 48:], state_ref[t + 1][:, :48]], axis=1) if (
                t + 1 < tiles
            ) else jnp.concatenate([here[:, 48:], jnp.zeros((COLS, 48), F32)], axis=1)
            new = old + keep * old + rate * (old + conv + bias)
            if step + 1 < ITERS:
                state_ref[t] = new * lane_scale(t, halo - 3)
            else:
                turned = new.T
                moved = None
                for piece in split3(turned):
                    part = jnp.dot(piece, order, preferred_element_type=F32)
                    moved = part if moved is None else moved + part
                for r in range(8):
                    out_ref[0, :, 8 * t + r, :] = moved[16 * r : 16 * r + 16]

    for start in range(ITERS):

        @pl.when(time == ITERS - start)
        def _():
            build_state(HALO - 3 * start)
            for step in range(start, ITERS):
                one_step(step)

    @pl.when(time == 0)
    def _():
        out_ref[0] = noise_ref[...]


def chain(
    start_noise, time_embed, keep_rate, denoise_rate, conv_first, conv_middle, conv_last, out_bias
):
    channels, rows, cols = start_noise.shape
    tm_size = lax.axis_size("tm")
    space_size = lax.axis_size("space")
    vmem = pl.BlockSpec(memory_space=pltpu.VMEM)
    shape = jax.ShapeDtypeStruct

    far = pl.pallas_call(
        pack_kernel,
        out_shape=pltpu.VMEM((3, cols), F32),
        in_specs=[vmem] * 3,
        out_specs=vmem,
    )(time_embed, keep_rate.reshape(1, 1), denoise_rate.reshape(1, 1))

    def swapped(value, first):
        pairs = [(i, i + 1) for i in range(first, space_size - 1, 2)]
        pairs += [(0, space_size - 1)] if first else []
        return lax.ppermute(value, "space", pairs + [(j, i) for i, j in pairs])

    def exchanged(apart):
        return lax.ppermute(far, "tm", [(t, t ^ apart) for t in range(tm_size)])

    start_noise, far = lax.optimization_barrier((start_noise, far))
    two = exchanged(2)
    near = swapped(start_noise, 0)
    across = swapped(start_noise, 1)
    one = exchanged(1)
    three = exchanged(3)

    w1, wm, w3, bias = pl.pallas_call(
        weights_kernel,
        out_shape=(
            pltpu.VMEM((4, 256, 256), BF16),
            pltpu.VMEM((1536, 256), BF16),
            pltpu.VMEM((4, 256, 256), BF16),
            pltpu.VMEM((1, COLS), F32),
        ),
        in_specs=[vmem] * 4,
        out_specs=(vmem,) * 4,
    )(jnp.swapaxes(conv_first, 1, 2), conv_middle, conv_last, out_bias.reshape(1, channels))

    total = rows + 2 * HALO
    pairs = (total - 2) // 2

    def body(*refs):
        chain_kernel(tm_size, space_size, rows, *refs)

    return pl.pallas_call(
        body,
        out_shape=shape((1, channels, rows, cols), F32),
        in_specs=[vmem] * 10,
        out_specs=vmem,
        scratch_shapes=[
            pltpu.VMEM((pl.cdiv(total, 8), COLS, COLS), F32),
            pltpu.VMEM((pl.cdiv(total, 8), PAD, COLS), BF16),
            pltpu.VMEM((pl.cdiv(total, 8), PAD, COLS), BF16),
            pltpu.VMEM((pairs, PAD, 256), BF16),
            pltpu.VMEM((pairs - 1, COLS, 256), BF16),
        ],
        compiler_params=pltpu.CompilerParams(vmem_limit_bytes=48 << 20),
    )(start_noise, two, near, across, one, three, bias, w1, wm, w3)


def solution(mesh):
    placed = (
        P(None, ("groups", "space"), None),
        P("tm", None),
        P("tm"),
        P("tm"),
        P(),
        P(),
        P(),
        P(),
    )
    return jax.shard_map(
        chain
        if mesh.shape["tm"] == ITERS + 1 and mesh.shape["space"] % 2 == 0
        else picard,
        mesh=mesh,
        in_specs=placed,
        out_specs=P("tm", None, ("groups", "space"), None),
        check_vma=False,
    )
```

```python
import jax
import jax.numpy as jnp
from jax import lax
from jax.experimental import pallas as pl
from jax.experimental.pallas import tpu as pltpu
from jax.sharding import PartitionSpec as P

ITERS = 3
HALO = 3 * ITERS
BF16 = jnp.bfloat16
F32 = jnp.float32


def padded(value, sides, width):
    for axis, dim in sides:
        count, length = (lax.axis_size(axis), value.shape[dim])
        up = [(i, (i + 1) % count) for i in range(count - 1)]
        down = [(j, i) for i, j in up]
        last = lax.slice_in_dim(value, length - width, length, axis=dim)
        initial = lax.slice_in_dim(value, 0, width, axis=dim)
        before = lax.ppermute(last, axis, up)
        after = lax.ppermute(initial, axis, down)
        value = jnp.concatenate([before, value, after], axis=dim)
    return value


def carried_in(part, axis):
    place = lax.axis_index(axis)
    gathered = lax.all_gather(part, axis)
    earlier = jnp.arange(gathered.shape[0]) < place
    return jnp.sum(jnp.where(earlier[:, None, None, None], gathered, 0.0), axis=0)


def convolve(field, taps):
    kernel = taps.reshape((3, 3, taps.shape[1], taps.shape[2]))
    result = lax.conv_general_dilated(
        field[None],
        kernel,
        (1, 1),
        ((0, 0), (1, 1)),
        dimension_numbers=("NCHW", "HWOI", "NCHW"),
        preferred_element_type=F32,
    )
    return result[0]


def inside_rows(margin, count, tile_rows):
    glob_row = lax.axis_index("space") * tile_rows - margin + jnp.arange(count, dtype=jnp.int32)
    valid = (glob_row >= 0) & (glob_row < tile_rows * lax.axis_size("space"))
    return valid.astype(F32)[None, :, None]


def picard(
    start_noise, time_embed, keep_rate, denoise_rate, conv_first, conv_middle, conv_last, out_bias
):
    tile_rows = start_noise.shape[1]
    embed = time_embed[0][:, None, None]
    keep = keep_rate[0]
    rate = denoise_rate[0]
    bias = out_bias[:, None, None]
    state = start_noise
    for step in range(ITERS):
        inputs = state.astype(BF16)
        extended = padded(inputs, (("space", 1),), 3)
        first = jax.nn.silu(convolve(extended, conv_first) + embed)
        first = (first * inside_rows(2, tile_rows + 4, tile_rows)).astype(BF16)
        second = jax.nn.silu(convolve(first, conv_middle))
        second = (second * inside_rows(1, tile_rows + 2, tile_rows)).astype(BF16)
        last = convolve(second, conv_last)
        denoised = state + last + bias
        drift = keep * state + rate * denoised
        state = start_noise + carried_in(drift, "tm")
    return state[None]


COLS = 128
GRAIN = 16
PAD = COLS + 2 * GRAIN


def pack_kernel(embed_ref, keep_ref, rate_ref, out_ref):
    out_ref[0:1] = embed_ref[...]
    out_ref[1:2] = jnp.broadcast_to(keep_ref[...], (1, COLS))
    out_ref[2:3] = jnp.broadcast_to(rate_ref[...], (1, COLS))


def weights_kernel(
    first_ref, middle_ref, last_ref, bias_in_ref, w1_ref, wm_ref, w3_ref, bias_ref
):
    bias_ref[...] = jnp.concatenate([bias_in_ref[...]] * 8, axis=1)
    halves = [first_ref[tap] * BF16(0.5) for tap in range(9)]
    none = jnp.zeros((16, 128), BF16)
    for place in range(4):
        for lanes in range(8):
            k = (lanes - 2 * place) % 8
            for out in range(2):
                for part in range(2):
                    a = k % 4 - out
                    b = 2 if part else k // 4
                    used = 0 <= a < 3 and not (part and k >= 4)
                    w1_ref[
                        place,
                        pl.ds(128 * part + 16 * lanes, 16),
                        pl.ds(128 * out, 128),
                    ] = halves[3 * a + b] if used else none
    zero = jnp.zeros((128, 128), BF16)
    for tap in range(9):
        a, b = divmod(tap, 3)
        block = (middle_ref[tap].astype(F32).T * 0.5).astype(BF16)
        for out in range(2):
            wm_ref[pl.ds(512 * b + 128 * (out + a), 128), pl.ds(128 * out, 128)] = block
    for b in range(3):
        wm_ref[pl.ds(512 * b + 384, 128), pl.ds(0, 128)] = zero
        wm_ref[pl.ds(512 * b, 128), pl.ds(128, 128)] = zero
    for place in range(4):
        for row in range(2):
            for part in range(2):
                parts = []
                for lanes in range(8):
                    k = (lanes - 2 * (place - 1)) % 8
                    a = row + 2 - k % 4
                    b = 2 if part else k // 4
                    if 0 <= a < 3 and not (part and k >= 4):
                        parts.append(last_ref[3 * a + b].astype(F32))
                    else:
                        parts.append(jnp.zeros((16, 128), F32))
                block = jnp.concatenate(parts, axis=0).T.astype(BF16)
                w3_ref[place, pl.ds(128 * row, 128), pl.ds(128 * part, 128)] = block


def split3(value):
    high = value.astype(BF16)
    rest = value - high.astype(F32)
    mid = rest.astype(BF16)
    low = (rest - mid.astype(F32)).astype(BF16)
    return high, mid, low


def shifted_rows(grain, by):
    row = lax.broadcasted_iota(jnp.int32, grain.shape, 0)
    if by > 0:
        return jnp.where(row == 0, 0.0, pltpu.roll(grain, 1, 0))
    return jnp.where(row == GRAIN - 1, 0.0, pltpu.roll(grain, GRAIN - 1, 0))


def half_silu(half):
    return half * jnp.tanh(half) + half


def chain_kernel(
    tm_size,
    space_size,
    rows,
    noise_ref,
    two_ref,
    near_ref,
    across_ref,
    one_ref,
    three_ref,
    bias_ref,
    w1_ref,
    wm_ref,
    w3_ref,
    out_ref,
    state_ref,
    zb_ref,
    zr_ref,
    first_ref,
    second_ref,
):
    time = lax.axis_index("tm")
    tile = lax.axis_index("space")
    even = tile % 2 == 0
    top = (tile > 0).astype(F32)
    bottom = (tile < space_size - 1).astype(F32)

    w_new = lax.broadcasted_iota(jnp.int32, (COLS, COLS), 0)
    w_old = lax.broadcasted_iota(jnp.int32, (COLS, COLS), 1)
    order = jnp.where(w_old == (w_new % GRAIN) * 8 + w_new // GRAIN, 1.0, 0.0).astype(BF16)
    lane = lax.broadcasted_iota(jnp.int32, (1, COLS), 1)
    lane_row = lane // 16

    def row_scale(rel):
        if rel < 0:
            return top
        if rel >= rows:
            return bottom
        return None

    def lane_scale(tile_index, halo):
        rel = lane_row + (8 * tile_index - halo)
        return jnp.where(rel < 0, top, jnp.where(rel >= rows, bottom, 1.0))

    def build_state(halo):
        total = rows + 2 * halo
        for t in range(pl.cdiv(total, 8)):
            parts = []
            for e in range(8 * t, 8 * t + 8):
                if e < halo:
                    row = rows - halo + e
                    parts.append(jnp.where(even, across_ref[:, row, :], near_ref[:, row, :]))
                elif e < halo + rows:
                    parts.append(noise_ref[:, e - halo, :])
                elif e < total:
                    row = e - halo - rows
                    parts.append(jnp.where(even, near_ref[:, row, :], across_ref[:, row, :]))
                else:
                    parts.append(jnp.zeros((16, COLS), F32))
            block = jnp.concatenate(parts, axis=0)
            moved = lax.dot_general(
                jnp.concatenate([order] * 3, axis=1),
                jnp.concatenate(split3(block), axis=1),
                (((1,), (1,)), ((), ())),
                preferred_element_type=F32,
            )
            state_ref[t] = moved * lane_scale(t, halo)

    bias = bias_ref[...]
    params = [
        three_ref[...],
        two_ref[...],
        jnp.where(time == 2, three_ref[...], one_ref[...]),
    ]

    def masked(value, pair, margin):
        halves = []
        scales = [row_scale(2 * pair + i - margin) for i in range(2)]
        if scales[0] is None and scales[1] is None:
            return value
        for i in range(2):
            half = value[:, 128 * i : 128 * (i + 1)]
            halves.append(half if scales[i] is None else half * scales[i])
        return jnp.concatenate(halves, axis=1)

    def keep_first(value, pair, margin):
        value = masked(half_silu(value), pair, margin)
        first_ref[pair, GRAIN : GRAIN + COLS, :] = value.astype(BF16)
        first_ref[pair, 0:GRAIN, :] = shifted_rows(value[COLS - GRAIN :], 1).astype(BF16)
        first_ref[pair, GRAIN + COLS :, :] = shifted_rows(value[:GRAIN], -1).astype(BF16)

    def one_step(step):
        halo = HALO - 3 * step
        count = rows + 2 * halo
        tiles = pl.cdiv(count, 8)
        pairs = (count - 2) // 2
        embed = params[step][0:1] * 0.5
        embed = jnp.concatenate([embed, embed], axis=1)
        keep = params[step][1:2]
        rate = params[step][2:3]

        def padded_tile(ref, t, z):
            ref[t, GRAIN : GRAIN + COLS, :] = z.astype(BF16)
            ref[t, 0:GRAIN, :] = shifted_rows(z[COLS - GRAIN :], 1).astype(BF16)
            ref[t, GRAIN + COLS :, :] = shifted_rows(z[:GRAIN], -1).astype(BF16)

        for t in range(tiles):
            padded_tile(zb_ref, t, state_ref[t])
            padded_tile(zr_ref, t, pltpu.roll(state_ref[t], 64, 1))

        for pair in range(pairs):
            t, place = divmod(pair, 4)
            here = [zb_ref[t, GRAIN * b : GRAIN * b + COLS, :] for b in range(3)]
            turned = zr_ref[t, GRAIN : GRAIN + COLS, :]
            if place < 3:
                window = (lane >= 32 * place) & (lane < 32 * place + 64)
                lhs = [jnp.where(window, here[0], turned), here[2]]
            else:
                after = [zb_ref[t + 1, GRAIN * b : GRAIN * b + COLS, :] for b in (0, 2)]
                mixed = jnp.where(lane < 64, turned, zr_ref[t + 1, GRAIN : GRAIN + COLS, :])
                lhs = [
                    jnp.where(lane < 32, after[0], jnp.where(lane < 96, mixed, here[0])),
                    jnp.where(lane < 64, after[1], here[2]),
                ]
            out = jnp.dot(
                jnp.concatenate(lhs, axis=1), w1_ref[place], preferred_element_type=F32
            )
            keep_first(out + embed, pair, halo - 1)

        for pair in range(pairs - 1):
            lhs = jnp.concatenate(
                [
                    first_ref[pair + i, GRAIN * b : GRAIN * b + COLS, :]
                    for b in range(3)
                    for i in range(2)
                ],
                axis=1,
            )
            out = jnp.dot(lhs, wm_ref[...], preferred_element_type=F32)
            second_ref[pair] = masked(half_silu(out), pair, halo - 2).astype(BF16)

        reach = [
            jnp.dot(second_ref[pair], w3_ref[pair % 4], preferred_element_type=F32)
            for pair in range(pairs - 1)
        ]
        low = lane < 64

        def spread(t, part):
            got = [
                reach[p][:, COLS * part : COLS * (part + 1)]
                if p < pairs - 1
                else jnp.zeros((COLS, COLS), F32)
                for p in range(4 * t, 4 * t + 5)
            ]
            proper = jnp.where(low, got[1], got[3]) + jnp.where(
                lane < 32, got[0], jnp.where(lane < 96, got[2], got[4])
            )
            if part == 1:
                return proper, None
            other = jnp.where(low, got[3], got[1]) + jnp.where(
                (lane < 32) | (lane >= 96), got[2], jnp.where(low, got[4], got[0])
            )
            return proper, pltpu.roll(other, 64, 1)

        for t in range(pl.cdiv(count - 6, 8)):
            left, centre = spread(t, 0)
            right, _ = spread(t, 1)
            left = jnp.concatenate(
                [shifted_rows(left[COLS - GRAIN :], 1), left[: COLS - GRAIN]], axis=0
            )
            right = jnp.concatenate([right[GRAIN:], shifted_rows(right[:GRAIN], -1)], axis=0)
            conv = left + centre + right
            here = state_ref[t]
            old = jnp.concatenate([here[:, 48:], state_ref[t + 1][:, :48]], axis=1) if (
                t + 1 < tiles
            ) else jnp.concatenate([here[:, 48:], jnp.zeros((COLS, 48), F32)], axis=1)
            new = old + keep * old + rate * (old + conv + bias)
            if step + 1 < ITERS:
                state_ref[t] = new * lane_scale(t, halo - 3)
            else:
                turned = new.T
                moved = jnp.dot(
                    jnp.concatenate(split3(turned), axis=1),
                    jnp.concatenate([order] * 3, axis=0),
                    preferred_element_type=F32,
                )
                for r in range(8):
                    out_ref[0, :, 8 * t + r, :] = moved[16 * r : 16 * r + 16]

    for start in range(ITERS):

        @pl.when(time == ITERS - start)
        def _():
            build_state(HALO - 3 * start)
            for step in range(start, ITERS):
                one_step(step)

    @pl.when(time == 0)
    def _():
        out_ref[0] = noise_ref[...]


def chain(
    start_noise, time_embed, keep_rate, denoise_rate, conv_first, conv_middle, conv_last, out_bias
):
    channels, rows, cols = start_noise.shape
    tm_size = lax.axis_size("tm")
    space_size = lax.axis_size("space")
    vmem = pl.BlockSpec(memory_space=pltpu.VMEM)
    shape = jax.ShapeDtypeStruct

    far = pl.pallas_call(
        pack_kernel,
        out_shape=pltpu.VMEM((3, cols), F32),
        in_specs=[vmem] * 3,
        out_specs=vmem,
    )(time_embed, keep_rate.reshape(1, 1), denoise_rate.reshape(1, 1))

    def swapped(value, first):
        pairs = [(i, i + 1) for i in range(first, space_size - 1, 2)]
        pairs += [(0, space_size - 1)] if first else []
        return lax.ppermute(value, "space", pairs + [(j, i) for i, j in pairs])

    def exchanged(apart):
        return lax.ppermute(far, "tm", [(t, t ^ apart) for t in range(tm_size)])

    start_noise, far = lax.optimization_barrier((start_noise, far))
    two = exchanged(2)
    near = swapped(start_noise, 0)
    across = swapped(start_noise, 1)
    one = exchanged(1)
    three = exchanged(3)

    w1, wm, w3, bias = pl.pallas_call(
        weights_kernel,
        out_shape=(
            pltpu.VMEM((4, 256, 256), BF16),
            pltpu.VMEM((1536, 256), BF16),
            pltpu.VMEM((4, 256, 256), BF16),
            pltpu.VMEM((1, COLS), F32),
        ),
        in_specs=[vmem] * 4,
        out_specs=(vmem,) * 4,
    )(jnp.swapaxes(conv_first, 1, 2), conv_middle, conv_last, out_bias.reshape(1, channels))

    total = rows + 2 * HALO
    pairs = (total - 2) // 2

    def body(*refs):
        chain_kernel(tm_size, space_size, rows, *refs)

    return pl.pallas_call(
        body,
        out_shape=shape((1, channels, rows, cols), F32),
        in_specs=[vmem] * 10,
        out_specs=vmem,
        scratch_shapes=[
            pltpu.VMEM((pl.cdiv(total, 8), COLS, COLS), F32),
            pltpu.VMEM((pl.cdiv(total, 8), PAD, COLS), BF16),
            pltpu.VMEM((pl.cdiv(total, 8), PAD, COLS), BF16),
            pltpu.VMEM((pairs, PAD, 256), BF16),
            pltpu.VMEM((pairs - 1, COLS, 256), BF16),
        ],
        compiler_params=pltpu.CompilerParams(vmem_limit_bytes=48 << 20),
    )(start_noise, two, near, across, one, three, bias, w1, wm, w3)


def solution(mesh):
    placed = (
        P(None, ("groups", "space"), None),
        P("tm", None),
        P("tm"),
        P("tm"),
        P(),
        P(),
        P(),
        P(),
    )
    return jax.shard_map(
        chain
        if mesh.shape["tm"] == ITERS + 1 and mesh.shape["space"] % 2 == 0
        else picard,
        mesh=mesh,
        in_specs=placed,
        out_specs=P("tm", None, ("groups", "space"), None),
        check_vma=False,
    )
```
